32 devices in a mesh: gy: 8 (over z, core), gz: 4 (over y, x).
Axes of the slice: x: 2, y: 2, z: 4, core: 2. Of those that a mesh axis runs over, the one named last changes fastest.
Arguments:
- state_field: bfloat16 [11, 64, 256, 512], P(None, 'gz', 'gy'), may hold values from -100 to 100, as said below
- start_factor: float32 [512, 64], replicated, may hold values from -6 to 6
Outputs:
- factor_one: float32 [512, 64], replicated
- mode_two_gram: float32 [256, 256], P('gy')
The draws below stay inside these ranges and needn't reach their ends.
Inputs may be any that keep to these rules, and one draw needn't show every extreme that they name: `state_field`: Real-valued field of full rank along every mode.
All inputs are finite; a program needn't handle non-finite values.
Results may differ from the reference program's by a relative error of at most 0.00052.
Values may be sent and summed in bfloat16 or wider, within the bound.
A program may use at most 64 MiB of HBM per device.

```python
import math
import jax
import jax.numpy as jnp
from jax import lax

N1 = 512
NV = 11
R1 = 64
ITERS = 6
N2 = 256
N3 = 64


def draw_state_field(key, part):
    keys = jax.random.split(key, 5)
    shape = (NV, N3, N2, N1)
    noise = jnp.clip(jax.random.normal(keys[0], shape, jnp.float32), -6.0, 6.0)
    ranks = jax.random.permutation(keys[1], N1).astype(jnp.float32)
    decay = 10.0 ** (-ranks / N1)
    depth_scale = jnp.exp(jax.random.uniform(keys[2], (N3,), jnp.float32, math.log(0.3), math.log(3.0)))
    cross_scale = jnp.exp(jax.random.uniform(keys[4], (N2,), jnp.float32, math.log(0.3), math.log(3.0)))
    base = noise * decay * cross_scale[:, None] * depth_scale[:, None, None]
    mixer = jax.random.permutation(keys[3], N1)
    return (base + 0.7 * jnp.take(base, mixer, axis=3)).astype(jnp.bfloat16)


def normal_values(own_key, extent, scale, reach, held_as=jnp.bfloat16):
    drawn = scale * jax.random.normal(own_key, extent, jnp.float32)
    return jnp.clip(drawn, min=-reach, max=reach).astype(held_as)


def setup_inputs(seed: int = 0) -> dict:
    splits = jax.random.split(jax.random.key(seed), 3)
    return {
        "state_field": draw_state_field(jax.random.fold_in(splits[2], 71), 0),
        "start_factor": normal_values(splits[1], (N1, R1), 1.0, 6.0, jnp.float32),
    }


def orthonormalize(images):
    cross_gram = jnp.dot(images.T, images, precision=lax.Precision.HIGHEST)
    lower_tri = jnp.linalg.cholesky(cross_gram)
    return lax.linalg.triangular_solve(lower_tri, images, left_side=False, lower=True, transpose_a=True)

def reference(state_field, start_factor):
    mode_gram = jnp.zeros((N1, N1), jnp.float32)
    for variable in range(NV):
        flattened = state_field[variable].astype(jnp.float32).reshape(-1, N1)
        mode_gram = mode_gram + lax.dot_general(flattened, flattened, (((0,), (0,)), ((), ())), precision=lax.Precision.HIGHEST)
    factor_one = start_factor
    for iteration in range(ITERS):
        images = jnp.dot(mode_gram, factor_one, precision=lax.Precision.HIGHEST)
        factor_one = orthonormalize(images)
    narrow = factor_one.astype(jnp.bfloat16).astype(jnp.float32)
    second = jnp.zeros((N2, N2), jnp.float32)
    for variable in range(NV):
        slab = state_field[variable].astype(jnp.float32)
        shrunk = jnp.einsum('kji,ir->jkr', slab, narrow, precision=lax.Precision.HIGHEST).astype(jnp.bfloat16)
        matrix = shrunk.astype(jnp.float32).reshape(N2, -1)
        second = second + lax.dot_general(matrix, matrix, (((1,), (1,)), ((), ())), precision=lax.Precision.HIGHEST)
    return (factor_one, second / (NV * N3 * R1))
```

```python
import functools

import jax
import jax.numpy as jnp
from jax import lax
from jax.experimental import pallas as pl
from jax.experimental.pallas import tpu as pltpu
from jax.sharding import PartitionSpec as P

ITERS = 6
AHEAD = 1
MESH = pl.DeviceIdType.MESH
LANES = 128
VMEM = pl.BlockSpec(memory_space=pltpu.VMEM)
ANY = pl.BlockSpec(memory_space=pl.ANY)
NT = (((1,), (1,)), ((), ()))


def greet(partners):
    barrier = pltpu.get_barrier_semaphore()
    for partner in partners:
        pl.semaphore_signal(barrier, inc=1, device_id=partner, device_id_type=MESH)
    pl.semaphore_wait(barrier, len(partners))


def send(src, dst, send_sem, recv_sem, device):
    copy = pltpu.make_async_remote_copy(
        src_ref=src, dst_ref=dst, send_sem=send_sem, recv_sem=recv_sem,
        device_id=device, device_id_type=MESH,
    )
    copy.start()
    return copy


def sum_kernel(ny, nz, chunk, g_ref, out_ref, packed, got1, held, got2, mid, got3, full,
               s1, r1, s2, r2, s3, r3, s4, r4, s5, r5, s6, r6):
    gy, gz = lax.axis_index("gy"), lax.axis_index("gz")
    depth = ny // 2
    zi, core = gy // 2, gy % 2
    rows2 = depth * chunk
    partner = (gy + 1 - 2 * core, gz)
    planes = [lax.rem(gz + o, nz) for o in range(nz)]
    stacks = [lax.rem(zi + o, depth) for o in range(depth)]

    def part(half, g):
        return pl.ds(pl.multiple_of((half * nz + g) * rows2, 8), rows2)

    n = g_ref.shape[0] // LANES
    blocks = [(i, j) for i in range(n) for j in range(i, n)]
    for k, (i, j) in enumerate(blocks):
        packed[k * LANES:(k + 1) * LANES, :] = g_ref[i * LANES:(i + 1) * LANES, j * LANES:(j + 1) * LANES]
    used = len(blocks) * LANES
    if used < packed.shape[0]:
        packed[used:, :] = jnp.zeros((packed.shape[0] - used, LANES), jnp.float32)

    greet([partner] + [(gy, g) for g in planes[1:]] + [(2 * q + core, gz) for q in stacks[1:]])

    order = list(range(1, nz)) + [0]
    copies = []
    first = {}
    for o in order:
        first[o] = send(packed.at[part(1 - core, planes[o])], got1.at[o], s1.at[o], r1.at[o], partner)
    second = {}
    for o in order:
        first[o].wait_recv()
        held[o] = packed[part(core, planes[o]), :] + got1[o]
        if o:
            second[o] = send(held.at[o], got2.at[o], s2.at[o], r2.at[o], (gy, planes[o]))
    total = held[0]
    for o in range(1, nz):
        second[o].wait_recv()
        total = total + got2[o]
    mid[...] = total
    third = {}
    for o in range(1, depth):
        rows = pl.ds(pl.multiple_of(stacks[o] * chunk, 8), chunk)
        third[o] = send(mid.at[rows], got3.at[o], s3.at[o], r3.at[o], (2 * stacks[o] + core, gz))
    piece = mid[pl.ds(pl.multiple_of(zi * chunk, 8), chunk), :]
    for o in range(1, depth):
        third[o].wait_recv()
        piece = piece + got3[o]
    mine = pl.ds(pl.multiple_of((core * nz + gz) * rows2 + zi * chunk, 8), chunk)
    full[mine, :] = piece
    fourth = {}
    for o in range(1, depth):
        fourth[o] = send(full.at[mine], full.at[mine], s4.at[o], r4.at[o], (2 * stacks[o] + core, gz))
    for o in range(1, depth):
        fourth[o].wait_recv()
    own = part(core, gz)
    fifth, sixth = {}, {}
    for o in range(1, nz):
        fifth[o] = send(full.at[own], full.at[own], s5.at[o], r5.at[o], (gy, planes[o]))
    sixth[0] = send(full.at[own], full.at[own], s6.at[0], r6.at[0], partner)
    for o in range(1, nz):
        fifth[o].wait_recv()
        came = part(core, lax.rem(gz + nz - o, nz))
        sixth[o] = send(full.at[came], full.at[came], s6.at[o], r6.at[o], partner)
    for o in range(nz):
        sixth[o].wait_recv()
    for group in (first, second, third, fourth, fifth, sixth):
        for copy in group.values():
            copy.wait_send()
    for k, (i, j) in enumerate(blocks):
        block = full[k * LANES:(k + 1) * LANES, :]
        out_ref[i * LANES:(i + 1) * LANES, j * LANES:(j + 1) * LANES] = block
        if i != j:
            out_ref[j * LANES:(j + 1) * LANES, i * LANES:(i + 1) * LANES] = block.T


def sum_over_devices(partial_gram):
    ny, nz = lax.axis_size("gy"), lax.axis_size("gz")
    n = partial_gram.shape[0] // LANES
    used = n * (n + 1) // 2 * LANES
    devices = ny * nz
    chunk = -(-used // (8 * devices)) * 8
    depth = ny // 2
    rows2 = depth * chunk
    f32 = jnp.float32
    dma = pltpu.SemaphoreType.DMA
    return pl.pallas_call(
        functools.partial(sum_kernel, ny, nz, chunk),
        out_shape=jax.ShapeDtypeStruct(partial_gram.shape, f32),
        in_specs=[VMEM], out_specs=VMEM,
        scratch_shapes=[
            pltpu.VMEM((chunk * devices, LANES), f32),
            pltpu.VMEM((nz, rows2, LANES), f32),
            pltpu.VMEM((nz, rows2, LANES), f32),
            pltpu.VMEM((nz, rows2, LANES), f32),
            pltpu.VMEM((rows2, LANES), f32),
            pltpu.VMEM((depth, chunk, LANES), f32),
            pltpu.VMEM((chunk * devices, LANES), f32),
        ] + [dma((nz,))] * 4 + [dma((depth,))] * 4 + [dma((nz,))] * 4,
        compiler_params=pltpu.CompilerParams(collective_id=0, has_side_effects=True),
        name="sum_gram",
    )(partial_gram)


def split(value):
    high = value.astype(jnp.bfloat16)
    rest = value - high.astype(jnp.float32)
    mid = rest.astype(jnp.bfloat16)
    low = (rest - mid.astype(jnp.float32)).astype(jnp.bfloat16)
    return high, mid, low


def dot(a, b, dims=(((1,), (0,)), ((), ()))):
    return lax.dot_general(a, b, dims, preferred_element_type=jnp.float32)


def rows_of(tile, k):
    return jnp.broadcast_to(tile[k:k + 1, :], tile.shape)


def lanes_of(tile, k):
    return jnp.take_along_axis(tile, jnp.full(tile.shape, k, jnp.int32), axis=1, mode="promise_in_bounds")


def inverse_lower(c):
    r1 = c.shape[0]
    nb = r1 // 8
    wide = 2 * r1
    row = lax.broadcasted_iota(jnp.int32, (r1, r1), 0)
    col = lax.broadcasted_iota(jnp.int32, (r1, r1), 1)
    whole = jnp.concatenate([c, (row == col).astype(jnp.float32)], axis=1)
    m = [whole[8 * i:8 * i + 8, :] for i in range(nb)]
    sub = lax.broadcasted_iota(jnp.int32, (8, wide), 0)
    lane = lax.broadcasted_iota(jnp.int32, (8, wide), 1)
    diag = [lanes_of(m[0], k) for k in range(8)]
    root = lax.rsqrt(rows_of(diag[0], 0))
    unit = root * root
    scale = jnp.where(lane < r1, unit, root)
    diag = [v * unit for v in diag]
    result = []
    for b in range(nb):
        cols = [[diag[k]] + [lanes_of(m[i], 8 * b + k) for i in range(b + 1, nb)] for k in range(8)]
        after = [lanes_of(m[b + 1], 8 * (b + 1) + k) for k in range(8)] if b + 1 < nb else []
        if b == 0:
            cols = [v[:1] + [x * unit for x in v[1:]] for v in cols]
            after = [x * unit for x in after]
            m = [x * scale for x in m]
        done = None
        for k in range(0, 8, 2):
            x, y = cols[k], cols[k + 1]
            p, q = x[0], y[0]
            a, e, d = rows_of(p, k), rows_of(p, k + 1), rows_of(q, k + 1)
            r = lax.rsqrt(a * d - e * e)
            inv = r * r
            g0, h0 = d * p - e * q, a * q - e * p
            ai, ei, di = a * inv, e * inv, d * inv
            ratio = [(g0 * inv, h0 * inv)]
            ratio += [(di * v - ei * w, ai * w - ei * v) for v, w in zip(x[1:], y[1:])]
            for k2 in range(k + 2, 8):
                s, t = rows_of(p, k2), rows_of(q, k2)
                new = [v - (g * s + h * t) for v, (g, h) in zip(cols[k2], ratio)]
                if k2 < k + 4:
                    new[0] = cols[k2][0] - (g0 * s + h0 * t) * inv
                cols[k2] = new
            for k2, v in enumerate(after):
                g, h = ratio[1]
                after[k2] = v - (g * rows_of(x[1], k2) + h * rows_of(y[1], k2))
            u, w = rows_of(m[b], k), rows_of(m[b], k + 1)
            ra = lax.rsqrt(a)
            fresh = jnp.where(sub == k, u * ra, (w - (e * (ra * ra)) * u) * (a * ra * r))
            done = fresh if done is None else jnp.where(sub < k, done, fresh)
            for i in range(b, nb):
                g, h = ratio[i - b]
                m[i] = m[i] - (g * u + h * w)
        result.append(done[:, r1:])
        diag = after
    return jnp.concatenate(result, axis=0)


def times_gram(a1, a2, a3, g1, g2, g3):
    r1 = a1.shape[0]
    t1 = dot(jnp.concatenate([a1, a2, a3], axis=0), g1[...])
    t2 = dot(jnp.concatenate([a1, a2], axis=0), g2[...])
    t3 = dot(a1, g3[...])
    return t1[:r1] + ((t1[r1:2 * r1] + t2[:r1]) + (t1[2 * r1:] + t2[r1:] + t3))


def iteration(g1, g2, g3, held, step, carry):
    r1 = held.shape[0]
    a1, a2, a3 = split(held[...])
    c = dot(a1, a1, NT) + (
        dot(a1, a2, NT) + dot(a2, a1, NT) + (dot(a2, a2, NT) + dot(a1, a3, NT) + dot(a3, a1, NT))
    )
    last = step == ITERS - 1
    b = split(times_gram(a1, a2, a3, g1, g2, g3))
    stack = jnp.concatenate([jnp.where(last, x, y) for x, y in zip((a1, a2, a3), b)], axis=0)
    w1, w2, w3 = split(inverse_lower(c))
    none = jnp.zeros_like(w1)
    t = dot(
        jnp.concatenate(
            [
                jnp.concatenate([w1, w1, w1], axis=1),
                jnp.concatenate([w2, w2, none], axis=1),
                jnp.concatenate([w3, none, none], axis=1),
            ],
            axis=0,
        ),
        stack,
    )
    held[...] = t[:r1] + (t[r1:2 * r1] + t[2 * r1:])
    return carry


def iterate_kernel(g_ref, f_ref, out_ref, g1, g2, g3, held):
    g1[...], g2[...], g3[...] = split(g_ref[...])
    held[...] = times_gram(*split(f_ref[...].T), g1, g2, g3)
    lax.fori_loop(0, ITERS, functools.partial(iteration, g1, g2, g3, held), 0)
    out_ref[...] = held[...].T


def iterate(mode_gram, start_factor):
    n, r1 = start_factor.shape
    return pl.pallas_call(
        iterate_kernel,
        out_shape=jax.ShapeDtypeStruct((n, r1), jnp.float32),
        in_specs=[VMEM, VMEM], out_specs=VMEM,
        scratch_shapes=[pltpu.VMEM((n, n), jnp.bfloat16)] * 3 + [pltpu.VMEM((r1, n), jnp.float32)],
        name="subspace",
    )(mode_gram, start_factor)


def whole_kernel(ny, nz, chunk, jb, ahead, scale, x_ref, f_ref, factor_ref, out_ref,
                 io, xs, acc, packed, got1, held, got2, mid, got3, full, g1, g2, g3, basis, weights,
                 raw, mine, z, gram, got4, part, got5, last,
                 xsem, s1, r1, s2, r2, s3, r3, s4, r4, s5, r5, s6, r6, sr, rr,
                 sa, ra, sb, rb, sc, rc, sd, rd):
    gy, gz = lax.axis_index("gy"), lax.axis_index("gz")
    depth = ny // 2
    zi, core = gy // 2, gy % 2
    partner = (gy + 1 - 2 * core, gz)
    planes = [lax.rem(gz + o, nz) for o in range(nz)]
    stacks = [lax.rem(zi + p, depth) for p in range(depth)]
    peers = [lax.rem(gy + o, ny) for o in range(ny)]
    rows = mine.shape[1]
    early = ahead * jb
    n1 = x_ref.shape[2]
    copies = []

    barrier = pltpu.get_barrier_semaphore()
    greeted = [(p, gz) for p in peers[1:]] + [(gy, g) for g in planes[1:]]
    for device in greeted:
        pl.semaphore_signal(barrier, inc=1, device_id=device, device_id_type=MESH)

    def load(o):
        src = x_ref.at[:, pl.ds(pl.multiple_of(peers[o] * rows, 8), rows)]
        return pltpu.make_async_copy(src, xs.at[o], xsem.at[o])

    loads = [load(o) for o in range(ny)]
    for copy in loads:
        copy.start()
    start = pltpu.make_async_copy(f_ref, basis, io.at[0])
    start.start()

    size = 2 * LANES
    for o in range(ny):
        loads[o].wait()
        for i in range(0, n1, size):
            left = xs[o, :, :, i:i + size].reshape(2 * rows, size)
            right = xs[o, :, :, i:].reshape(2 * rows, n1 - i)
            value = dot(left, right, (((0,), (0,)), ((), ())))
            if o:
                acc[i:i + size, i:] += value
            else:
                acc[i:i + size, i:] = value

    n = n1 // LANES
    blocks = [(i, j) for i in range(n) for j in range(i, n)]
    for k, (i, j) in enumerate(blocks):
        packed[k * LANES:(k + 1) * LANES, :] = acc[i * LANES:(i + 1) * LANES, j * LANES:(j + 1) * LANES]
    used = len(blocks) * LANES
    if used < packed.shape[0]:
        packed[used:, :] = jnp.zeros((packed.shape[0] - used, LANES), jnp.float32)

    pl.semaphore_wait(barrier, len(greeted))

    unit = nz * chunk

    def span(half, q):
        return pl.ds(pl.multiple_of((half * depth + q) * unit, 8), unit)

    def spot(half, q, g):
        return pl.ds(pl.multiple_of((half * depth + q) * unit + g * chunk, 8), chunk)

    order = list(range(depth - 1, 0, -1)) + [0]
    first, second, third = {}, {}, {}
    for p in order:
        first[p] = send(packed.at[span(1 - core, stacks[p])], got1.at[p], s1.at[p], r1.at[p], partner)
    for p in order:
        first[p].wait_recv()
        held[p] = packed[span(core, stacks[p]), :] + got1[p]
        for o in range(1, nz):
            rows_o = pl.ds(pl.multiple_of(planes[o] * chunk, 8), chunk)
            second[p, o] = send(held.at[p, rows_o], got2.at[p, o], s2.at[p, o], r2.at[p, o], (gy, planes[o]))
    piece = None
    for p in order:
        total = held[p, pl.ds(pl.multiple_of(gz * chunk, 8), chunk), :]
        for o in range(1, nz):
            second[p, o].wait_recv()
            total = total + got2[p, o]
        if p:
            mid[p] = total
            third[p] = send(mid.at[p], got3.at[p], s3.at[p], r3.at[p], (2 * stacks[p] + core, gz))
        else:
            piece = total
    for p in range(1, depth):
        third[p].wait_recv()
        piece = piece + got3[p]
    own = spot(core, zi, gz)
    full[own, :] = piece
    fourth, fifth, sixth = {}, {}, {}
    for p in range(1, depth):
        fourth[p] = send(full.at[own], full.at[own], s4.at[p], r4.at[p], (2 * stacks[p] + core, gz))
    came = [lax.rem(zi + depth - p, depth) for p in range(depth)]
    for p in range(depth):
        if p:
            fourth[p].wait_recv()
        here = spot(core, came[p], gz)
        for o in range(1, nz):
            fifth[p, o] = send(full.at[here], full.at[here], s5.at[p, o], r5.at[p, o], (gy, planes[o]))
    for p in range(depth):
        for o in range(1, nz):
            fifth[p, o].wait_recv()
        here = span(core, came[p])
        sixth[p] = send(full.at[here], full.at[here], s6.at[p], r6.at[p], partner)
    for p in range(depth):
        sixth[p].wait_recv()

    sent = {}
    if ahead:
        for o in range(1, ny):
            sent[o] = send(xs.at[o, :, pl.ds(0, early)], raw.at[gy], sr.at[o], rr.at[o], (peers[o], gz))

    for k, (i, j) in enumerate(blocks):
        block = full[k * LANES:(k + 1) * LANES, :]
        for a, b, value in ((i, j, block), (j, i, block.T))[:1 if i == j else 2]:
            where = (slice(a * LANES, (a + 1) * LANES), slice(b * LANES, (b + 1) * LANES))
            g1[where], g2[where], g3[where] = split(value)
    start.wait()
    basis[...] = times_gram(*split(basis[...]), g1, g2, g3)
    lax.fori_loop(0, ITERS, functools.partial(iteration, g1, g2, g3, basis), 0)
    factor = basis[...]
    leave = pltpu.make_async_copy(basis, factor_ref, io.at[1])
    leave.start()
    narrow = factor.T.astype(jnp.bfloat16)
    empty = jnp.zeros_like(narrow)
    weights[0] = jnp.concatenate([narrow, empty], axis=1)
    weights[1] = jnp.concatenate([empty, narrow], axis=1)

    def project(pair):
        return (dot(pair[0], weights[0]) + dot(pair[1], weights[1])).astype(jnp.bfloat16)

    across = {}
    far = list(range(ny // 2, ny)) + list(range(ny // 2 - 1, 0, -1))
    for o in far:
        mine[o, early:] = project(xs[o, :, early:])
        across[o] = send(
            mine.at[o, pl.ds(early, rows - early)], z.at[gy, pl.ds(early, rows - early)],
            sa.at[o], ra.at[o], (peers[o], gz),
        )
    z[gy] = project(xs[0])
    if ahead:
        for o in range(1, ny):
            sent[o].wait_recv()
            source = lax.rem(gy + ny - o, ny)
            z[source, :early] = project(raw[source])
    for o in range(1, ny):
        across[o].wait_recv()
    wide = jnp.concatenate(
        [z[:, t * jb:(t + 1) * jb, :].reshape(ny * jb, LANES) for t in range(rows // jb)], axis=1
    )
    gram[...] = dot(wide, wide, NT).reshape(gram.shape)
    planar, rowwise, final = {}, {}, {}
    far = far + [0]
    for o in far:
        for g in range(1, nz):
            planar[o, g] = send(
                gram.at[peers[o], planes[g]], got4.at[o, g], sb.at[o, g], rb.at[o, g], (gy, planes[g])
            )
    for o in far:
        total = gram[peers[o], gz]
        for g in range(1, nz):
            planar[o, g].wait_recv()
            total = total + got4[o, g]
        if o:
            part[o] = total
            rowwise[o] = send(part.at[o], got5.at[o], sc.at[o], rc.at[o], (peers[o], gz))
    for o in range(1, ny):
        rowwise[o].wait_recv()
        total = total + got5[o]
    last[gz] = total * scale
    for o in range(1, nz):
        final[o] = send(last.at[gz], last.at[gz], sd.at[o], rd.at[o], (gy, planes[o]))
    for o in range(1, nz):
        final[o].wait_recv()
    done = pltpu.make_async_copy(last, out_ref, io.at[2])
    done.start()
    for group in (first, second, third, fourth, fifth, sixth, sent, across, planar, rowwise, final):
        for copy in group.values():
            copy.wait_send()
    leave.wait()
    done.wait()


def deliver_kernel(a_ref, b_ref, c_ref, d_ref):
    c_ref[...] = a_ref[...]
    d_ref[...] = b_ref[...]


def deliver(a, b):
    shape = jax.ShapeDtypeStruct
    return pl.pallas_call(
        deliver_kernel, out_shape=(shape(a.shape, a.dtype), shape(b.shape, b.dtype)),
        in_specs=[VMEM, VMEM], out_specs=(VMEM, VMEM), name="deliver",
    )(a, b)


def whole(state_field, start_factor, divisor):
    ny, nz = lax.axis_size("gy"), lax.axis_size("gz")
    nv, nk, jb, n1 = state_field.shape
    r1 = start_factor.shape[1]
    half = nv * nk // 2
    rows = half // ny * jb
    ahead = AHEAD
    halves = state_field.reshape(2, half * jb, n1)
    n = n1 // LANES
    used = n * (n + 1) // 2 * LANES
    chunk = -(-used // (8 * ny * nz)) * 8
    depth = ny // 2
    unit = nz * chunk
    q, j2 = jb // nz, ny * jb
    f32, bf16 = jnp.float32, jnp.bfloat16
    dma = pltpu.SemaphoreType.DMA
    vmem = pltpu.VMEM
    factor, out = pl.pallas_call(
        functools.partial(whole_kernel, ny, nz, chunk, jb, ahead, 1.0 / divisor),
        out_shape=(jax.ShapeDtypeStruct((r1, n1), f32), jax.ShapeDtypeStruct((nz, q, j2), f32)),
        in_specs=[ANY, ANY], out_specs=(ANY, ANY),
        scratch_shapes=[
            dma((3,)),
            vmem((ny, 2, rows, n1), bf16),
            vmem((n1, n1), f32),
            vmem((chunk * ny * nz, LANES), f32),
            vmem((depth, unit, LANES), f32),
            vmem((depth, unit, LANES), f32),
            vmem((depth, nz, chunk, LANES), f32),
            vmem((depth, chunk, LANES), f32),
            vmem((depth, chunk, LANES), f32),
            vmem((chunk * ny * nz, LANES), f32),
            vmem((n1, n1), bf16), vmem((n1, n1), bf16), vmem((n1, n1), bf16),
            vmem((r1, n1), f32),
            vmem((2, n1, LANES), bf16),
            vmem((ny, 2, max(ahead, 1) * jb, n1), bf16),
            vmem((ny, rows, LANES), bf16),
            vmem((ny, rows, LANES), bf16),
            vmem((ny, nz, q, j2), f32),
            vmem((ny, nz, q, j2), f32),
            vmem((ny, q, j2), f32),
            vmem((ny, q, j2), f32),
            vmem((nz, q, j2), f32),
            dma((ny,)),
        ] + [dma((depth,))] * 2 + [dma((depth, nz))] * 2 + [dma((depth,))] * 4 + [dma((depth, nz))] * 2
        + [dma((depth,))] * 2 + [dma((ny,))] * 4 + [dma((ny, nz))] * 2 + [dma((ny,))] * 2 + [dma((nz,))] * 2,
        compiler_params=pltpu.CompilerParams(
            collective_id=1, has_side_effects=True, vmem_limit_bytes=56 * 2**20
        ),
        name="whole",
    )(halves, start_factor.T)
    factor, out = deliver(factor, out)
    return factor.T, out.reshape(jb, j2)


def second_gram_plain(state_field, narrow, divisor):
    shrunk = jnp.einsum(
        "vkji,ir->jvkr", state_field, narrow, preferred_element_type=jnp.float32
    ).astype(jnp.bfloat16)
    matrix = shrunk.reshape(shrunk.shape[0], -1)
    columns = lax.all_to_all(matrix, "gy", split_axis=1, concat_axis=0, tiled=True)
    partial_two = lax.psum_scatter(dot(columns, columns, NT), "gy", scatter_dimension=0, tiled=True)
    return lax.psum(partial_two, "gz") / divisor


def per_device(state_field, start_factor):
    ny, nz = lax.axis_size("gy"), lax.axis_size("gz")
    nv, nk, jb, n1 = state_field.shape
    r1 = start_factor.shape[1]
    divisor = nv * nk * nz * r1
    if (nv * nk) % (2 * ny) == 0 and jb % (8 * nz) == 0 and 2 * r1 == LANES and n1 % (2 * LANES) == 0:
        return whole(state_field, start_factor, divisor)
    flattened = state_field.reshape(-1, n1)
    partial_value = dot(flattened, flattened, (((0,), (0,)), ((), ())))
    factor_one = iterate(sum_over_devices(partial_value), start_factor)
    return (factor_one, second_gram_plain(state_field, factor_one.astype(jnp.bfloat16), divisor))


def solution(mesh):
    placed = (P(None, "gz", "gy", None), P())
    return jax.shard_map(
        per_device, mesh=mesh, in_specs=placed, out_specs=(P(), P("gy", None)), check_vma=False
    )
```

```python
import functools

import jax
import jax.numpy as jnp
from jax import lax
from jax.experimental import pallas as pl
from jax.experimental.pallas import tpu as pltpu
from jax.sharding import PartitionSpec as P

ITERS = 6
AHEAD = 1
MESH = pl.DeviceIdType.MESH
LANES = 128
VMEM = pl.BlockSpec(memory_space=pltpu.VMEM)
ANY = pl.BlockSpec(memory_space=pl.ANY)
NT = (((1,), (1,)), ((), ()))


def greet(partners):
    barrier = pltpu.get_barrier_semaphore()
    for partner in partners:
        pl.semaphore_signal(barrier, inc=1, device_id=partner, device_id_type=MESH)
    pl.semaphore_wait(barrier, len(partners))


def send(src, dst, send_sem, recv_sem, device):
    copy = pltpu.make_async_remote_copy(
        src_ref=src, dst_ref=dst, send_sem=send_sem, recv_sem=recv_sem,
        device_id=device, device_id_type=MESH,
    )
    copy.start()
    return copy


def settle(view, sem):
    pltpu.make_async_copy(view, view, sem).wait()


def sum_kernel(ny, nz, chunk, g_ref, out_ref, packed, got1, held, got2, mid, got3, full,
               s1, r1, s2, r2, s3, r3, s4, r4, s5, r5, s6, r6):
    gy, gz = lax.axis_index("gy"), lax.axis_index("gz")
    depth = ny // 2
    zi, core = gy // 2, gy % 2
    rows2 = depth * chunk
    partner = (gy + 1 - 2 * core, gz)
    planes = [lax.rem(gz + o, nz) for o in range(nz)]
    stacks = [lax.rem(zi + o, depth) for o in range(depth)]

    def part(half, g):
        return pl.ds(pl.multiple_of((half * nz + g) * rows2, 8), rows2)

    n = g_ref.shape[0] // LANES
    blocks = [(i, j) for i in range(n) for j in range(i, n)]
    for k, (i, j) in enumerate(blocks):
        packed[k * LANES:(k + 1) * LANES, :] = g_ref[i * LANES:(i + 1) * LANES, j * LANES:(j + 1) * LANES]
    used = len(blocks) * LANES
    if used < packed.shape[0]:
        packed[used:, :] = jnp.zeros((packed.shape[0] - used, LANES), jnp.float32)

    greet([partner] + [(gy, g) for g in planes[1:]] + [(2 * q + core, gz) for q in stacks[1:]])

    order = list(range(1, nz)) + [0]
    copies = []
    first = {}
    for o in order:
        first[o] = send(packed.at[part(1 - core, planes[o])], got1.at[o], s1.at[o], r1.at[o], partner)
    second = {}
    for o in order:
        first[o].wait_recv()
        held[o] = packed[part(core, planes[o]), :] + got1[o]
        if o:
            second[o] = send(held.at[o], got2.at[o], s2.at[o], r2.at[o], (gy, planes[o]))
    total = held[0]
    for o in range(1, nz):
        second[o].wait_recv()
        total = total + got2[o]
    mid[...] = total
    third = {}
    for o in range(1, depth):
        rows = pl.ds(pl.multiple_of(stacks[o] * chunk, 8), chunk)
        third[o] = send(mid.at[rows], got3.at[o], s3.at[o], r3.at[o], (2 * stacks[o] + core, gz))
    piece = mid[pl.ds(pl.multiple_of(zi * chunk, 8), chunk), :]
    for o in range(1, depth):
        third[o].wait_recv()
        piece = piece + got3[o]
    mine = pl.ds(pl.multiple_of((core * nz + gz) * rows2 + zi * chunk, 8), chunk)
    full[mine, :] = piece
    fourth = {}
    for o in range(1, depth):
        fourth[o] = send(full.at[mine], full.at[mine], s4.at[o], r4.at[o], (2 * stacks[o] + core, gz))
    for o in range(1, depth):
        fourth[o].wait_recv()
    own = part(core, gz)
    fifth, sixth = {}, {}
    for o in range(1, nz):
        fifth[o] = send(full.at[own], full.at[own], s5.at[o], r5.at[o], (gy, planes[o]))
    sixth[0] = send(full.at[own], full.at[own], s6.at[0], r6.at[0], partner)
    for o in range(1, nz):
        fifth[o].wait_recv()
        came = part(core, lax.rem(gz + nz - o, nz))
        sixth[o] = send(full.at[came], full.at[came], s6.at[o], r6.at[o], partner)
    for o in range(nz):
        sixth[o].wait_recv()
    for group in (first, second, third, fourth, fifth, sixth):
        for copy in group.values():
            copy.wait_send()
    for k, (i, j) in enumerate(blocks):
        block = full[k * LANES:(k + 1) * LANES, :]
        out_ref[i * LANES:(i + 1) * LANES, j * LANES:(j + 1) * LANES] = block
        if i != j:
            out_ref[j * LANES:(j + 1) * LANES, i * LANES:(i + 1) * LANES] = block.T


def sum_over_devices(partial_gram):
    ny, nz = lax.axis_size("gy"), lax.axis_size("gz")
    n = partial_gram.shape[0] // LANES
    used = n * (n + 1) // 2 * LANES
    devices = ny * nz
    chunk = -(-used // (8 * devices)) * 8
    depth = ny // 2
    rows2 = depth * chunk
    f32 = jnp.float32
    dma = pltpu.SemaphoreType.DMA
    return pl.pallas_call(
        functools.partial(sum_kernel, ny, nz, chunk),
        out_shape=jax.ShapeDtypeStruct(partial_gram.shape, f32),
        in_specs=[VMEM], out_specs=VMEM,
        scratch_shapes=[
            pltpu.VMEM((chunk * devices, LANES), f32),
            pltpu.VMEM((nz, rows2, LANES), f32),
            pltpu.VMEM((nz, rows2, LANES), f32),
            pltpu.VMEM((nz, rows2, LANES), f32),
            pltpu.VMEM((rows2, LANES), f32),
            pltpu.VMEM((depth, chunk, LANES), f32),
            pltpu.VMEM((chunk * devices, LANES), f32),
        ] + [dma((nz,))] * 4 + [dma((depth,))] * 4 + [dma((nz,))] * 4,
        compiler_params=pltpu.CompilerParams(collective_id=0, has_side_effects=True),
        name="sum_gram",
    )(partial_gram)


def split(value):
    high = value.astype(jnp.bfloat16)
    rest = value - high.astype(jnp.float32)
    mid = rest.astype(jnp.bfloat16)
    low = (rest - mid.astype(jnp.float32)).astype(jnp.bfloat16)
    return high, mid, low


def dot(a, b, dims=(((1,), (0,)), ((), ()))):
    return lax.dot_general(a, b, dims, preferred_element_type=jnp.float32)


def rows_of(tile, k):
    return jnp.broadcast_to(tile[k:k + 1, :], tile.shape)


def lanes_of(tile, k):
    return jnp.take_along_axis(tile, jnp.full(tile.shape, k, jnp.int32), axis=1, mode="promise_in_bounds")


def inverse_lower(c):
    r1 = c.shape[0]
    nb = r1 // 8
    wide = 2 * r1
    row = lax.broadcasted_iota(jnp.int32, (r1, r1), 0)
    col = lax.broadcasted_iota(jnp.int32, (r1, r1), 1)
    whole = jnp.concatenate([c, (row == col).astype(jnp.float32)], axis=1)
    m = [whole[8 * i:8 * i + 8, :] for i in range(nb)]
    sub = lax.broadcasted_iota(jnp.int32, (8, wide), 0)
    lane = lax.broadcasted_iota(jnp.int32, (8, wide), 1)
    diag = [lanes_of(m[0], k) for k in range(8)]
    root = lax.rsqrt(rows_of(diag[0], 0))
    unit = root * root
    scale = jnp.where(lane < r1, unit, root)
    diag = [v * unit for v in diag]
    result = []
    for b in range(nb):
        cols = [[diag[k]] + [lanes_of(m[i], 8 * b + k) for i in range(b + 1, nb)] for k in range(8)]
        after = [lanes_of(m[b + 1], 8 * (b + 1) + k) for k in range(8)] if b + 1 < nb else []
        if b == 0:
            cols = [v[:1] + [x * unit for x in v[1:]] for v in cols]
            after = [x * unit for x in after]
            m = [x * scale for x in m]
        done = None
        for k in range(0, 8, 2):
            x, y = cols[k], cols[k + 1]
            p, q = x[0], y[0]
            a, e, d = rows_of(p, k), rows_of(p, k + 1), rows_of(q, k + 1)
            r = lax.rsqrt(a * d - e * e)
            inv = r * r
            g0, h0 = d * p - e * q, a * q - e * p
            ai, ei, di = a * inv, e * inv, d * inv
            ratio = [(g0 * inv, h0 * inv)]
            ratio += [(di * v - ei * w, ai * w - ei * v) for v, w in zip(x[1:], y[1:])]
            for k2 in range(k + 2, 8):
                s, t = rows_of(p, k2), rows_of(q, k2)
                new = [v - (g * s + h * t) for v, (g, h) in zip(cols[k2], ratio)]
                if k2 < k + 4:
                    new[0] = cols[k2][0] - (g0 * s + h0 * t) * inv
                cols[k2] = new
            for k2, v in enumerate(after):
                g, h = ratio[1]
                after[k2] = v - (g * rows_of(x[1], k2) + h * rows_of(y[1], k2))
            u, w = rows_of(m[b], k), rows_of(m[b], k + 1)
            ra = lax.rsqrt(a)
            fresh = jnp.where(sub == k, u * ra, (w - (e * (ra * ra)) * u) * (a * ra * r))
            done = fresh if done is None else jnp.where(sub < k, done, fresh)
            for i in range(b, nb):
                g, h = ratio[i - b]
                m[i] = m[i] - (g * u + h * w)
        result.append(done[:, r1:])
        diag = after
    return jnp.concatenate(result, axis=0)


def times_gram(a1, a2, a3, g1, g2, g3):
    r1 = a1.shape[0]
    t1 = dot(jnp.concatenate([a1, a2, a3], axis=0), g1[...])
    t2 = dot(jnp.concatenate([a1, a2], axis=0), g2[...])
    t3 = dot(a1, g3[...])
    return t1[:r1] + ((t1[r1:2 * r1] + t2[:r1]) + (t1[2 * r1:] + t2[r1:] + t3))


def iteration(g1, g2, g3, held, step, carry):
    r1 = held.shape[0]
    a1, a2, a3 = split(held[...])
    c = dot(a1, a1, NT) + (
        dot(a1, a2, NT) + dot(a2, a1, NT) + (dot(a2, a2, NT) + dot(a1, a3, NT) + dot(a3, a1, NT))
    )
    last = step == ITERS - 1
    b = split(times_gram(a1, a2, a3, g1, g2, g3))
    stack = jnp.concatenate([jnp.where(last, x, y) for x, y in zip((a1, a2, a3), b)], axis=0)
    w1, w2, w3 = split(inverse_lower(c))
    none = jnp.zeros_like(w1)
    t = dot(
        jnp.concatenate(
            [
                jnp.concatenate([w1, w1, w1], axis=1),
                jnp.concatenate([w2, w2, none], axis=1),
                jnp.concatenate([w3, none, none], axis=1),
            ],
            axis=0,
        ),
        stack,
    )
    held[...] = t[:r1] + (t[r1:2 * r1] + t[2 * r1:])
    return carry


def iterate_kernel(g_ref, f_ref, out_ref, g1, g2, g3, held):
    g1[...], g2[...], g3[...] = split(g_ref[...])
    held[...] = times_gram(*split(f_ref[...].T), g1, g2, g3)
    lax.fori_loop(0, ITERS, functools.partial(iteration, g1, g2, g3, held), 0)
    out_ref[...] = held[...].T


def iterate(mode_gram, start_factor):
    n, r1 = start_factor.shape
    return pl.pallas_call(
        iterate_kernel,
        out_shape=jax.ShapeDtypeStruct((n, r1), jnp.float32),
        in_specs=[VMEM, VMEM], out_specs=VMEM,
        scratch_shapes=[pltpu.VMEM((n, n), jnp.bfloat16)] * 3 + [pltpu.VMEM((r1, n), jnp.float32)],
        name="subspace",
    )(mode_gram, start_factor)


def tiles_of(n):
    return [(i, j) for i in range(n) for j in range(i + 1, n)] + [(i, i) for i in range(n)]


def blocks_of(n):
    blocks = []
    for i, j in tiles_of(n // 2):
        blocks += [(2 * i + a, 2 * j + b) for a in range(2) for b in range(2) if i < j or a <= b]
    return blocks


def whole_kernel(ny, nz, chunk, jb, ahead, scale, x_ref, f_ref, factor_ref, out_ref,
                 io, xs, packed, got1, held, got2, mid, got3, full, g1, g2, g3, basis, weights,
                 raw, mine, z, gram, got4, part, got5, last,
                 xsem, left, r1, r2, r3, r4, r5, r6, rr, ra, rb, rc, rd):
    gy, gz = lax.axis_index("gy"), lax.axis_index("gz")
    depth = ny // 2
    zi, core = gy // 2, gy % 2
    partner = (gy + 1 - 2 * core, gz)
    planes = [lax.rem(gz + o, nz) for o in range(nz)]
    stacks = [lax.rem(zi + p, depth) for p in range(depth)]
    peers = [lax.rem(gy + o, ny) for o in range(ny)]
    rows = mine.shape[1]
    early = ahead * jb
    n1 = x_ref.shape[2]

    barrier = pltpu.get_barrier_semaphore()
    greeted = [(p, gz) for p in peers[1:]] + [(gy, g) for g in planes[1:]]
    for device in greeted:
        pl.semaphore_signal(barrier, inc=1, device_id=device, device_id_type=MESH)

    def load(o):
        src = x_ref.at[:, pl.ds(pl.multiple_of(peers[o] * rows, 8), rows)]
        return pltpu.make_async_copy(src, xs.at[o], xsem.at[2 * o // ny])

    loads = [load(o) for o in range(ny)]
    for copy in loads:
        copy.start()
    start = pltpu.make_async_copy(f_ref, basis, io.at[0])
    start.start()

    size = 2 * LANES
    n = n1 // LANES
    blocks = blocks_of(n)
    groups = len(blocks) // 2
    order = {block: k for k, block in enumerate(blocks)}
    wide_piece = LANES // nz
    small = wide_piece // depth

    def add_tile(i, j, low, high, start):
        deep = (high - low) * 2 * rows
        left = xs[low:high, :, :, i * size:(i + 1) * size].reshape(deep, size)
        right = xs[low:high, :, :, j * size:(j + 1) * size].reshape(deep, size)
        value = dot(left, right, (((0,), (0,)), ((), ())))
        for a in range(2):
            for b in range(2):
                k = order.get((2 * i + a, 2 * j + b))
                if k is not None:
                    block = value[a * LANES:(a + 1) * LANES, b * LANES:(b + 1) * LANES]
                    if start:
                        packed[k] = block
                    else:
                        packed[k] += block

    def pair_up(k):
        send(packed.at[2 * k + 1 - core], got1.at[k], left.at[0], r1.at[k], partner)

    def spread_plane(k):
        settle(got1.at[k], r1.at[k])
        held[k] = packed[2 * k + core] + got1[k]
        for o in range(1, nz):
            part_o = pl.ds(pl.multiple_of(planes[o] * wide_piece, 8), wide_piece)
            send(held.at[k, part_o], got2.at[k, o - 1], left.at[1], r2.at[k], (gy, planes[o]))

    tiles = tiles_of(n // 2)
    half_way = ny // 2
    for low in (0, half_way):
        settle(xs.at[pl.ds(low, half_way)], xsem.at[low // half_way])
        add_tile(*tiles[0], low, low + half_way, low == 0)
    pl.semaphore_wait(barrier, len(greeted))
    for k in range(2):
        pair_up(k)
    for i, j in tiles[1:]:
        for low in (0, half_way):
            add_tile(i, j, low, low + half_way, low == 0)
    for k in range(2, groups):
        pair_up(k)
    for k in range(groups):
        spread_plane(k)
    for k in range(groups):
        total = held[k, pl.ds(pl.multiple_of(gz * wide_piece, 8), wide_piece), :]
        settle(got2.at[k], r2.at[k])
        for o in range(1, nz):
            total = total + got2[k, o - 1]
        mid[k] = total
        for p in range(1, depth):
            part_p = pl.ds(pl.multiple_of(stacks[p] * small, 8), small)
            send(mid.at[k, part_p], got3.at[k, p - 1], left.at[2], r3.at[0], (2 * stacks[p] + core, gz))

    unit = nz * chunk

    def span(half, q):
        return pl.ds(pl.multiple_of((half * depth + q) * unit, 8), unit)

    def spot(half, q, g):
        return pl.ds(pl.multiple_of((half * depth + q) * unit + g * chunk, 8), chunk)

    base_row = (core * depth + zi) * unit + gz * chunk
    settle(got3, r3.at[0])
    for k in range(groups):
        piece = mid[k, pl.ds(pl.multiple_of(zi * small, 8), small), :]
        for p in range(1, depth):
            piece = piece + got3[k, p - 1]
        full[pl.ds(pl.multiple_of(base_row + k * small, 8), small), :] = piece
    own = spot(core, zi, gz)
    for p in range(1, depth):
        send(full.at[own], full.at[own], left.at[3], r4.at[p - 1], (2 * stacks[p] + core, gz))
    came = [lax.rem(zi + depth - p, depth) for p in range(depth)]
    for p in range(depth):
        if p:
            settle(full.at[pl.ds(0, chunk)], r4.at[p - 1])
        here = spot(core, came[p], gz)
        for o in range(1, nz):
            send(full.at[here], full.at[here], left.at[4], r5.at[p], (gy, planes[o]))
    for p in range(depth):
        settle(full.at[pl.ds(0, (nz - 1) * chunk)], r5.at[p])
        here = span(core, came[p])
        send(full.at[here], full.at[here], left.at[5], r6.at[0], partner)
    settle(full.at[pl.ds(0, depth * unit)], r6.at[0])

    far = list(range(ny // 2, ny)) + list(range(ny // 2 - 1, 0, -1))
    if ahead:
        for o in far:
            send(xs.at[o, :, pl.ds(0, early)], raw.at[gy], left.at[6], rr.at[0], (peers[o], gz))

    for k, (i, j) in enumerate(blocks):
        rows_k = [((k % 2 * depth + q) * nz + g) * chunk + k // 2 * small for g in range(nz) for q in range(depth)]
        block = jnp.concatenate([full[row:row + small, :] for row in rows_k], axis=0)
        for a, b, value in ((i, j, block), (j, i, block.T))[:1 if i == j else 2]:
            where = (slice(a * LANES, (a + 1) * LANES), slice(b * LANES, (b + 1) * LANES))
            g1[where], g2[where], g3[where] = split(value)
    start.wait()
    basis[...] = times_gram(*split(basis[...]), g1, g2, g3)
    lax.fori_loop(0, ITERS, functools.partial(iteration, g1, g2, g3, basis), 0)
    factor = basis[...]
    leave = pltpu.make_async_copy(basis, factor_ref, io.at[1])
    leave.start()
    narrow = factor.T.astype(jnp.bfloat16)
    empty = jnp.zeros_like(narrow)
    weights[0] = jnp.concatenate([narrow, empty], axis=1)
    weights[1] = jnp.concatenate([empty, narrow], axis=1)

    def project(pair):
        return (dot(pair[0], weights[0]) + dot(pair[1], weights[1])).astype(jnp.bfloat16)

    late = pl.ds(early, rows - early)
    for o in far:
        mine[o, early:] = project(xs[o, :, early:])
        send(mine.at[o, late], z.at[gy, late], left.at[7], ra.at[0], (peers[o], gz))
    z[gy] = project(xs[0])
    if ahead:
        settle(raw.at[pl.ds(0, ny - 1)], rr.at[0])
        for o in range(1, ny):
            source = lax.rem(gy + ny - o, ny)
            z[source, :early] = project(raw[source])
    settle(z.at[pl.ds(0, ny - 1), late], ra.at[0])
    wide = jnp.concatenate(
        [z[:, t * jb:(t + 1) * jb, :].reshape(ny * jb, LANES) for t in range(rows // jb)], axis=1
    )
    gram[...] = dot(wide, wide, NT).reshape(gram.shape)
    far = far + [0]
    for o in far:
        for g in range(1, nz):
            send(gram.at[peers[o], planes[g]], got4.at[o, g - 1], left.at[8], rb.at[o], (gy, planes[g]))
    for o in far:
        settle(got4.at[o], rb.at[o])
        total = gram[peers[o], gz]
        for g in range(1, nz):
            total = total + got4[o, g - 1]
        if o:
            part[o - 1] = total
            send(part.at[o - 1], got5.at[o - 1], left.at[9], rc.at[0], (peers[o], gz))
    settle(got5, rc.at[0])
    for o in range(1, ny):
        total = total + got5[o - 1]
    last[gz] = total * scale
    for o in range(1, nz):
        send(last.at[gz], last.at[gz], left.at[10], rd.at[0], (gy, planes[o]))
    settle(last.at[pl.ds(0, nz - 1)], rd.at[0])
    done = pltpu.make_async_copy(last, out_ref, io.at[2])
    done.start()
    gone = [
        got1, got2, got3, full.at[pl.ds(0, (depth - 1) * chunk)], full.at[pl.ds(0, depth * (nz - 1) * chunk)],
        full.at[pl.ds(0, depth * unit)], raw.at[pl.ds(0, ny - 1)], z.at[pl.ds(0, ny - 1), late], got4, got5,
        last.at[pl.ds(0, nz - 1)],
    ]
    for k, view in enumerate(gone):
        if ahead or k != 6:
            settle(view, left.at[k])
    leave.wait()
    done.wait()


def deliver_kernel(a_ref, b_ref, c_ref, d_ref):
    c_ref[...] = a_ref[...]
    d_ref[...] = b_ref[...]


def deliver(a, b):
    shape = jax.ShapeDtypeStruct
    return pl.pallas_call(
        deliver_kernel, out_shape=(shape(a.shape, a.dtype), shape(b.shape, b.dtype)),
        in_specs=[VMEM, VMEM], out_specs=(VMEM, VMEM), name="deliver",
    )(a, b)


def whole(state_field, start_factor, divisor):
    ny, nz = lax.axis_size("gy"), lax.axis_size("gz")
    nv, nk, jb, n1 = state_field.shape
    r1 = start_factor.shape[1]
    half = nv * nk // 2
    rows = half // ny * jb
    ahead = AHEAD
    halves = state_field.reshape(2, half * jb, n1)
    n = n1 // LANES
    groups = n * (n + 1) // 4
    depth = ny // 2
    small = LANES // (nz * depth)
    chunk = groups * small
    q, j2 = jb // nz, ny * jb
    f32, bf16 = jnp.float32, jnp.bfloat16
    dma = pltpu.SemaphoreType.DMA
    vmem = pltpu.VMEM
    factor, out = pl.pallas_call(
        functools.partial(whole_kernel, ny, nz, chunk, jb, ahead, 1.0 / divisor),
        out_shape=(jax.ShapeDtypeStruct((r1, n1), f32), jax.ShapeDtypeStruct((nz, q, j2), f32)),
        in_specs=[ANY, ANY], out_specs=(ANY, ANY),
        scratch_shapes=[
            dma((3,)),
            vmem((ny, 2, rows, n1), bf16),
            vmem((2 * groups, LANES, LANES), f32),
            vmem((groups, LANES, LANES), f32),
            vmem((groups, LANES, LANES), f32),
            vmem((groups, nz - 1, LANES // nz, LANES), f32),
            vmem((groups, LANES // nz, LANES), f32),
            vmem((groups, depth - 1, small, LANES), f32),
            vmem((chunk * ny * nz, LANES), f32),
            vmem((n1, n1), bf16), vmem((n1, n1), bf16), vmem((n1, n1), bf16),
            vmem((r1, n1), f32),
            vmem((2, n1, LANES), bf16),
            vmem((ny, 2, max(ahead, 1) * jb, n1), bf16),
            vmem((ny, rows, LANES), bf16),
            vmem((ny, rows, LANES), bf16),
            vmem((ny, nz, q, j2), f32),
            vmem((ny, nz - 1, q, j2), f32),
            vmem((ny - 1, q, j2), f32),
            vmem((ny - 1, q, j2), f32),
            vmem((nz, q, j2), f32),
            dma((2,)), dma((11,)), dma((groups,)), dma((groups,)), dma((1,)), dma((depth - 1,)), dma((depth,)),
            dma((1,)), dma((1,)), dma((1,)), dma((ny,)), dma((1,)), dma((1,)),
        ],
        compiler_params=pltpu.CompilerParams(
            collective_id=1, has_side_effects=True, vmem_limit_bytes=56 * 2**20
        ),
        name="whole",
    )(halves, start_factor.T)
    factor, out = deliver(factor, out)
    return factor.T, out.reshape(jb, j2)


def second_gram_plain(state_field, narrow, divisor):
    shrunk = jnp.einsum(
        "vkji,ir->jvkr", state_field, narrow, preferred_element_type=jnp.float32
    ).astype(jnp.bfloat16)
    matrix = shrunk.reshape(shrunk.shape[0], -1)
    columns = lax.all_to_all(matrix, "gy", split_axis=1, concat_axis=0, tiled=True)
    partial_two = lax.psum_scatter(dot(columns, columns, NT), "gy", scatter_dimension=0, tiled=True)
    return lax.psum(partial_two, "gz") / divisor


def per_device(state_field, start_factor):
    ny, nz = lax.axis_size("gy"), lax.axis_size("gz")
    nv, nk, jb, n1 = state_field.shape
    r1 = start_factor.shape[1]
    divisor = nv * nk * nz * r1
    halves = (nv * nk) % (2 * ny) == 0 and jb % (8 * nz) == 0 and 2 * r1 == LANES
    if halves and n1 % (4 * LANES) == 0 and ny % 4 == 0 and LANES % (4 * ny * nz) == 0:
        return whole(state_field, start_factor, divisor)
    flattened = state_field.reshape(-1, n1)
    partial_value = dot(flattened, flattened, (((0,), (0,)), ((), ())))
    factor_one = iterate(sum_over_devices(partial_value), start_factor)
    return (factor_one, second_gram_plain(state_field, factor_one.astype(jnp.bfloat16), divisor))


def solution(mesh):
    placed = (P(None, "gz", "gy", None), P())
    return jax.shard_map(
        per_device, mesh=mesh, in_specs=placed, out_specs=(P(), P("gy", None)), check_vma=False
    )
```

```python
import functools

import jax
import jax.numpy as jnp
from jax import lax
from jax.experimental import pallas as pl
from jax.experimental.pallas import tpu as pltpu
from jax.sharding import PartitionSpec as P

ITERS = 6
EARLY = (4, 5)
TWICE = (4, 5)
MESH = pl.DeviceIdType.MESH
LANES = 128
VMEM = pl.BlockSpec(memory_space=pltpu.VMEM)
ANY = pl.BlockSpec(memory_space=pl.ANY)
NT = (((1,), (1,)), ((), ()))


def greet(partners):
    barrier = pltpu.get_barrier_semaphore()
    for partner in partners:
        pl.semaphore_signal(barrier, inc=1, device_id=partner, device_id_type=MESH)
    pl.semaphore_wait(barrier, len(partners))


def send(src, dst, send_sem, recv_sem, device):
    copy = pltpu.make_async_remote_copy(
        src_ref=src, dst_ref=dst, send_sem=send_sem, recv_sem=recv_sem,
        device_id=device, device_id_type=MESH,
    )
    copy.start()
    return copy


def settle(view, sem):
    pltpu.make_async_copy(view, view, sem).wait()


def sum_kernel(ny, nz, chunk, g_ref, out_ref, packed, got1, held, got2, mid, got3, full,
               s1, r1, s2, r2, s3, r3, s4, r4, s5, r5, s6, r6):
    gy, gz = lax.axis_index("gy"), lax.axis_index("gz")
    depth = ny // 2
    zi, core = gy // 2, gy % 2
    rows2 = depth * chunk
    partner = (gy + 1 - 2 * core, gz)
    planes = [lax.rem(gz + o, nz) for o in range(nz)]
    stacks = [lax.rem(zi + o, depth) for o in range(depth)]

    def part(half, g):
        return pl.ds(pl.multiple_of((half * nz + g) * rows2, 8), rows2)

    n = g_ref.shape[0] // LANES
    blocks = [(i, j) for i in range(n) for j in range(i, n)]
    for k, (i, j) in enumerate(blocks):
        packed[k * LANES:(k + 1) * LANES, :] = g_ref[i * LANES:(i + 1) * LANES, j * LANES:(j + 1) * LANES]
    used = len(blocks) * LANES
    if used < packed.shape[0]:
        packed[used:, :] = jnp.zeros((packed.shape[0] - used, LANES), jnp.float32)

    greet([partner] + [(gy, g) for g in planes[1:]] + [(2 * q + core, gz) for q in stacks[1:]])

    order = list(range(1, nz)) + [0]
    copies = []
    first = {}
    for o in order:
        first[o] = send(packed.at[part(1 - core, planes[o])], got1.at[o], s1.at[o], r1.at[o], partner)
    second = {}
    for o in order:
        first[o].wait_recv()
        held[o] = packed[part(core, planes[o]), :] + got1[o]
        if o:
            second[o] = send(held.at[o], got2.at[o], s2.at[o], r2.at[o], (gy, planes[o]))
    total = held[0]
    for o in range(1, nz):
        second[o].wait_recv()
        total = total + got2[o]
    mid[...] = total
    third = {}
    for o in range(1, depth):
        rows = pl.ds(pl.multiple_of(stacks[o] * chunk, 8), chunk)
        third[o] = send(mid.at[rows], got3.at[o], s3.at[o], r3.at[o], (2 * stacks[o] + core, gz))
    piece = mid[pl.ds(pl.multiple_of(zi * chunk, 8), chunk), :]
    for o in range(1, depth):
        third[o].wait_recv()
        piece = piece + got3[o]
    mine = pl.ds(pl.multiple_of((core * nz + gz) * rows2 + zi * chunk, 8), chunk)
    full[mine, :] = piece
    fourth = {}
    for o in range(1, depth):
        fourth[o] = send(full.at[mine], full.at[mine], s4.at[o], r4.at[o], (2 * stacks[o] + core, gz))
    for o in range(1, depth):
        fourth[o].wait_recv()
    own = part(core, gz)
    fifth, sixth = {}, {}
    for o in range(1, nz):
        fifth[o] = send(full.at[own], full.at[own], s5.at[o], r5.at[o], (gy, planes[o]))
    sixth[0] = send(full.at[own], full.at[own], s6.at[0], r6.at[0], partner)
    for o in range(1, nz):
        fifth[o].wait_recv()
        came = part(core, lax.rem(gz + nz - o, nz))
        sixth[o] = send(full.at[came], full.at[came], s6.at[o], r6.at[o], partner)
    for o in range(nz):
        sixth[o].wait_recv()
    for group in (first, second, third, fourth, fifth, sixth):
        for copy in group.values():
            copy.wait_send()
    for k, (i, j) in enumerate(blocks):
        block = full[k * LANES:(k + 1) * LANES, :]
        out_ref[i * LANES:(i + 1) * LANES, j * LANES:(j + 1) * LANES] = block
        if i != j:
            out_ref[j * LANES:(j + 1) * LANES, i * LANES:(i + 1) * LANES] = block.T


def sum_over_devices(partial_gram):
    ny, nz = lax.axis_size("gy"), lax.axis_size("gz")
    n = partial_gram.shape[0] // LANES
    used = n * (n + 1) // 2 * LANES
    devices = ny * nz
    chunk = -(-used // (8 * devices)) * 8
    depth = ny // 2
    rows2 = depth * chunk
    f32 = jnp.float32
    dma = pltpu.SemaphoreType.DMA
    return pl.pallas_call(
        functools.partial(sum_kernel, ny, nz, chunk),
        out_shape=jax.ShapeDtypeStruct(partial_gram.shape, f32),
        in_specs=[VMEM], out_specs=VMEM,
        scratch_shapes=[
            pltpu.VMEM((chunk * devices, LANES), f32),
            pltpu.VMEM((nz, rows2, LANES), f32),
            pltpu.VMEM((nz, rows2, LANES), f32),
            pltpu.VMEM((nz, rows2, LANES), f32),
            pltpu.VMEM((rows2, LANES), f32),
            pltpu.VMEM((depth, chunk, LANES), f32),
            pltpu.VMEM((chunk * devices, LANES), f32),
        ] + [dma((nz,))] * 4 + [dma((depth,))] * 4 + [dma((nz,))] * 4,
        compiler_params=pltpu.CompilerParams(collective_id=0, has_side_effects=True),
        name="sum_gram",
    )(partial_gram)


def split(value):
    high = value.astype(jnp.bfloat16)
    rest = value - high.astype(jnp.float32)
    mid = rest.astype(jnp.bfloat16)
    low = (rest - mid.astype(jnp.float32)).astype(jnp.bfloat16)
    return high, mid, low


def dot(a, b, dims=(((1,), (0,)), ((), ()))):
    return lax.dot_general(a, b, dims, preferred_element_type=jnp.float32)


def rows_of(tile, k):
    return jnp.broadcast_to(tile[k:k + 1, :], tile.shape)


def lanes_of(tile, k):
    return jnp.take_along_axis(tile, jnp.full(tile.shape, k, jnp.int32), axis=1, mode="promise_in_bounds")


def inverse_lower(c):
    r1 = c.shape[0]
    nb = r1 // 8
    wide = 2 * r1
    row = lax.broadcasted_iota(jnp.int32, (r1, r1), 0)
    col = lax.broadcasted_iota(jnp.int32, (r1, r1), 1)
    whole = jnp.concatenate([c, (row == col).astype(jnp.float32)], axis=1)
    m = [whole[8 * i:8 * i + 8, :] for i in range(nb)]
    sub = lax.broadcasted_iota(jnp.int32, (8, wide), 0)
    lane = lax.broadcasted_iota(jnp.int32, (8, wide), 1)
    diag = [lanes_of(m[0], k) for k in range(8)]
    root = lax.rsqrt(rows_of(diag[0], 0))
    unit = root * root
    scale = jnp.where(lane < r1, unit, root)
    diag = [v * unit for v in diag]
    result = []
    for b in range(nb):
        cols = [[diag[k]] + [lanes_of(m[i], 8 * b + k) for i in range(b + 1, nb)] for k in range(8)]
        after = [lanes_of(m[b + 1], 8 * (b + 1) + k) for k in range(8)] if b + 1 < nb else []
        if b == 0:
            cols = [v[:1] + [x * unit for x in v[1:]] for v in cols]
            after = [x * unit for x in after]
            m = [x * scale for x in m]
        done = None
        for k in range(0, 8, 2):
            x, y = cols[k], cols[k + 1]
            p, q = x[0], y[0]
            a, e, d = rows_of(p, k), rows_of(p, k + 1), rows_of(q, k + 1)
            r = lax.rsqrt(a * d - e * e)
            inv = r * r
            g0, h0 = d * p - e * q, a * q - e * p
            ai, ei, di = a * inv, e * inv, d * inv
            ratio = [(g0 * inv, h0 * inv)]
            ratio += [(di * v - ei * w, ai * w - ei * v) for v, w in zip(x[1:], y[1:])]
            for k2 in range(k + 2, 8):
                s, t = rows_of(p, k2), rows_of(q, k2)
                new = [v - (g * s + h * t) for v, (g, h) in zip(cols[k2], ratio)]
                if k2 < k + 4:
                    new[0] = cols[k2][0] - (g0 * s + h0 * t) * inv
                cols[k2] = new
            for k2, v in enumerate(after):
                g, h = ratio[1]
                after[k2] = v - (g * rows_of(x[1], k2) + h * rows_of(y[1], k2))
            u, w = rows_of(m[b], k), rows_of(m[b], k + 1)
            ra = lax.rsqrt(a)
            fresh = jnp.where(sub == k, u * ra, (w - (e * (ra * ra)) * u) * (a * ra * r))
            done = fresh if done is None else jnp.where(sub < k, done, fresh)
            for i in range(b, nb):
                g, h = ratio[i - b]
                m[i] = m[i] - (g * u + h * w)
        result.append(done[:, r1:])
        diag = after
    return jnp.concatenate(result, axis=0)


def times_gram(a1, a2, a3, g1, g2, g3):
    r1 = a1.shape[0]
    t1 = dot(jnp.concatenate([a1, a2, a3], axis=0), g1[...])
    t2 = dot(jnp.concatenate([a1, a2], axis=0), g2[...])
    t3 = dot(a1, g3[...])
    return t1[:r1] + ((t1[r1:2 * r1] + t2[:r1]) + (t1[2 * r1:] + t2[r1:] + t3))


def iteration(g1, g2, g3, held, step, carry):
    r1 = held.shape[0]
    a1, a2, a3 = split(held[...])
    p1 = dot(jnp.concatenate([a1, a2, a3], axis=0), a1, NT)
    p2 = dot(jnp.concatenate([a1, a2], axis=0), a2, NT)
    p3 = dot(a1, a3, NT)
    c = p1[:r1] + (p2[:r1] + p1[r1:2 * r1] + (p2[r1:] + p3 + p1[2 * r1:]))
    last = step == ITERS - 1
    b = split(times_gram(a1, a2, a3, g1, g2, g3))
    stack = jnp.concatenate([jnp.where(last, x, y) for x, y in zip((a1, a2, a3), b)], axis=0)
    w1, w2, w3 = split(inverse_lower(c))
    none = jnp.zeros_like(w1)
    t = dot(
        jnp.concatenate(
            [
                jnp.concatenate([w1, w1, w1], axis=1),
                jnp.concatenate([w2, w2, none], axis=1),
                jnp.concatenate([w3, none, none], axis=1),
            ],
            axis=0,
        ),
        stack,
    )
    held[...] = t[:r1] + (t[r1:2 * r1] + t[2 * r1:])
    return carry


def iterate_kernel(g_ref, f_ref, out_ref, g1, g2, g3, held):
    g1[...], g2[...], g3[...] = split(g_ref[...])
    held[...] = times_gram(*split(f_ref[...].T), g1, g2, g3)
    lax.fori_loop(0, ITERS, functools.partial(iteration, g1, g2, g3, held), 0)
    out_ref[...] = held[...].T


def iterate(mode_gram, start_factor):
    n, r1 = start_factor.shape
    return pl.pallas_call(
        iterate_kernel,
        out_shape=jax.ShapeDtypeStruct((n, r1), jnp.float32),
        in_specs=[VMEM, VMEM], out_specs=VMEM,
        scratch_shapes=[pltpu.VMEM((n, n), jnp.bfloat16)] * 3 + [pltpu.VMEM((r1, n), jnp.float32)],
        name="subspace",
    )(mode_gram, start_factor)


def batches_of(groups):
    early = groups - 2
    return [list(range(early)), list(range(early, groups))] if early > 0 else [list(range(groups))]


def tiles_of(n):
    return [(i, j) for i in range(n) for j in range(i + 1, n)] + [(i, i) for i in range(n)]


def blocks_of(n):
    blocks = []
    for i, j in tiles_of(n // 2):
        blocks += [(2 * i + a, 2 * j + b) for a in range(2) for b in range(2) if i < j or a <= b]
    return blocks


def whole_kernel(ny, nz, jb, scale, x_ref, f_ref, factor_ref, out_ref,
                 io, xs, packed, got1, held, got2, mid, got3, full, g1, g2, g3, basis, weights,
                 raw, more, mine, z, gram, got4, part, got5, last,
                 xsem, left, r1, r2, r3, r4, r5, r6, rr, ra, rb, rc, rd):
    gy, gz = lax.axis_index("gy"), lax.axis_index("gz")
    depth = ny // 2
    zi, core = gy // 2, gy % 2
    partner = (gy + 1 - 2 * core, gz)
    planes = [lax.rem(gz + o, nz) for o in range(nz)]
    stacks = [lax.rem(zi + p, depth) for p in range(depth)]
    peers = [lax.rem(gy + o, ny) for o in range(ny)]
    rows = mine.shape[1]
    soon = [o for o in EARLY if 0 < o < ny]
    twice = [o for o in TWICE if 0 < o < ny]
    once = [o for o in range(1, ny) if o not in twice]
    first_rows, next_rows = pl.ds(0, jb), pl.ds(jb, jb)
    n1 = x_ref.shape[2]

    barrier = pltpu.get_barrier_semaphore()
    greeted = [(p, gz) for p in peers[1:]] + [(gy, g) for g in planes[1:]]
    for device in greeted:
        pl.semaphore_signal(barrier, inc=1, device_id=device, device_id_type=MESH)

    def load(o):
        src = x_ref.at[:, pl.ds(pl.multiple_of(peers[o] * rows, 8), rows)]
        return pltpu.make_async_copy(src, xs.at[o], xsem.at[2 * o // ny])

    loads = [load(o) for o in range(ny)]
    for copy in loads:
        copy.start()
    start = pltpu.make_async_copy(f_ref, basis, io.at[0])
    start.start()

    size = 2 * LANES
    n = n1 // LANES
    blocks = blocks_of(n)
    groups = len(blocks) // 2
    order = {block: k for k, block in enumerate(blocks)}
    wide_piece = LANES // nz
    small = wide_piece // depth
    batches = batches_of(groups)
    batch_of = {k: b for b, batch in enumerate(batches) for k in batch}

    def add_tile(i, j, low, high, start):
        deep = (high - low) * 2 * rows
        left = xs[low:high, :, :, i * size:(i + 1) * size].reshape(deep, size)
        right = xs[low:high, :, :, j * size:(j + 1) * size].reshape(deep, size)
        value = dot(left, right, (((0,), (0,)), ((), ())))
        for a in range(2):
            for b in range(2):
                k = order.get((2 * i + a, 2 * j + b))
                if k is not None:
                    block = value[a * LANES:(a + 1) * LANES, b * LANES:(b + 1) * LANES]
                    if start:
                        packed[k] = block
                    else:
                        packed[k] += block

    def pair_up(k):
        send(packed.at[2 * k + 1 - core], got1.at[k], left.at[0], r1.at[k], partner)

    def spread_plane(k):
        settle(got1.at[k], r1.at[k])
        held[k] = packed[2 * k + core] + got1[k]
        for o in range(1, nz):
            part_o = pl.ds(pl.multiple_of(planes[o] * wide_piece, 8), wide_piece)
            send(held.at[k, part_o], got2.at[k, o - 1], left.at[1], r2.at[k], (gy, planes[o]))

    tiles = tiles_of(n // 2)
    half_way = ny // 2
    for low in (0, half_way):
        settle(xs.at[pl.ds(low, half_way)], xsem.at[low // half_way])
        add_tile(*tiles[0], low, low + half_way, low == 0)
    pl.semaphore_wait(barrier, len(greeted))
    def send_raw(o):
        send(xs.at[o, :, first_rows], raw.at[gy], left.at[6], rr.at[0], (peers[o], gz))

    for k in range(2):
        pair_up(k)
    for o in soon:
        send_raw(o)
    for i, j in tiles[1:]:
        for low in (0, half_way):
            add_tile(i, j, low, low + half_way, low == 0)
    for k in range(2, groups):
        pair_up(k)
    for k in range(groups):
        spread_plane(k)
    for k in range(groups):
        total = held[k, pl.ds(pl.multiple_of(gz * wide_piece, 8), wide_piece), :]
        settle(got2.at[k], r2.at[k])
        for o in range(1, nz):
            total = total + got2[k, o - 1]
        mid[k] = total
        for p in range(1, depth):
            part_p = pl.ds(pl.multiple_of(stacks[p] * small, 8), small)
            send(mid.at[k, part_p], got3.at[k, p - 1], left.at[2], r3.at[batch_of[k]], (2 * stacks[p] + core, gz))

    pieces = 2 * depth * nz

    def span(b, half, q, g=0, count=nz):
        chunk = len(batches[b]) * small
        start = batches[b][0] * small * pieces
        return pl.ds(pl.multiple_of(start + ((half * depth + q) * nz + g) * chunk, 8), count * chunk)

    def some(b, count):
        return full.at[pl.ds(0, count * len(batches[b]) * small)]

    for b, batch in enumerate(batches):
        settle(got3.at[pl.ds(batch[0], len(batch))], r3.at[b])
        total = mid[batch[0]:batch[-1] + 1, pl.ds(pl.multiple_of(zi * small, 8), small), :]
        for p in range(1, depth):
            total = total + got3[batch[0]:batch[-1] + 1, p - 1]
        own = span(b, core, zi, gz, 1)
        full[own, :] = total.reshape(len(batch) * small, LANES)
        for p in range(1, depth):
            send(full.at[own], full.at[own], left.at[3], r4.at[b, p - 1], (2 * stacks[p] + core, gz))
    came = [lax.rem(zi + depth - p, depth) for p in range(depth)]
    for b in range(len(batches)):
        for p in range(depth):
            if p:
                settle(some(b, 1), r4.at[b, p - 1])
            here = span(b, core, came[p], gz, 1)
            for o in range(1, nz):
                send(full.at[here], full.at[here], left.at[4], r5.at[b, p], (gy, planes[o]))
    for b in range(len(batches)):
        for p in range(depth):
            settle(some(b, nz - 1), r5.at[b, p])
            here = span(b, core, came[p])
            send(full.at[here], full.at[here], left.at[5], r6.at[0], partner)
    rows_full = pieces * groups * small
    settle(full.at[pl.ds(0, rows_full // 2)], r6.at[0])

    far = list(range(ny // 2, ny)) + list(range(ny // 2 - 1, 0, -1))
    for o in far:
        if o not in soon:
            send_raw(o)
    for o in twice:
        send(xs.at[o, :, next_rows], more.at[gy], left.at[11], rr.at[1], (peers[o], gz))

    for k, (i, j) in enumerate(blocks):
        batch = batches[batch_of[k // 2]]
        chunk = len(batch) * small
        at = batch[0] * small * pieces + (k // 2 - batch[0]) * small
        rows_k = [at + ((k % 2 * depth + q) * nz + g) * chunk for g in range(nz) for q in range(depth)]
        block = jnp.concatenate([full[row:row + small, :] for row in rows_k], axis=0)
        for a, b, value in ((i, j, block), (j, i, block.T))[:1 if i == j else 2]:
            where = (slice(a * LANES, (a + 1) * LANES), slice(b * LANES, (b + 1) * LANES))
            g1[where], g2[where], g3[where] = split(value)
    start.wait()
    basis[...] = times_gram(*split(basis[...]), g1, g2, g3)
    lax.fori_loop(0, ITERS, functools.partial(iteration, g1, g2, g3, basis), 0)
    factor = basis[...]
    leave = pltpu.make_async_copy(basis, factor_ref, io.at[1])
    leave.start()
    narrow = factor.T.astype(jnp.bfloat16)
    empty = jnp.zeros_like(narrow)
    weights[0] = jnp.concatenate([narrow, empty], axis=1)
    weights[1] = jnp.concatenate([empty, narrow], axis=1)

    def project(pair):
        return (dot(pair[0], weights[0]) + dot(pair[1], weights[1])).astype(jnp.bfloat16)

    ranges = {o: pl.ds(2 * jb, rows - 2 * jb) if o in twice else pl.ds(jb, rows - jb) for o in far}
    for o in far:
        late, kind = ranges[o], int(o in twice)
        mine[o, late] = project(xs[o, :, late])
        send(mine.at[o, late], z.at[gy, late], left.at[12 if kind else 7], ra.at[kind], (peers[o], gz))
    z[gy] = project(xs[0])
    settle(raw.at[pl.ds(0, ny - 1)], rr.at[0])
    for o in range(1, ny):
        z[peers[o], first_rows] = project(raw[peers[o]])
    if twice:
        settle(more.at[pl.ds(0, len(twice))], rr.at[1])
    for o in twice:
        source = lax.rem(gy + ny - o, ny)
        z[source, next_rows] = project(more[source])
    whole_once = z.at[pl.ds(0, len(once)), pl.ds(jb, rows - jb)]
    settle(whole_once, ra.at[0])
    whole_twice = z.at[pl.ds(0, max(len(twice), 1)), pl.ds(2 * jb, rows - 2 * jb)]
    if twice:
        settle(whole_twice, ra.at[1])
    wide = jnp.concatenate(
        [z[:, t * jb:(t + 1) * jb, :].reshape(ny * jb, LANES) for t in range(rows // jb)], axis=1
    )
    gram[...] = dot(wide, wide, NT).reshape(gram.shape)
    far = far + [0]
    for o in far:
        for g in range(1, nz):
            send(gram.at[peers[o], planes[g]], got4.at[o, g - 1], left.at[8], rb.at[o], (gy, planes[g]))
    for o in far:
        settle(got4.at[o], rb.at[o])
        total = gram[peers[o], gz]
        for g in range(1, nz):
            total = total + got4[o, g - 1]
        if o:
            part[o - 1] = total
            send(part.at[o - 1], got5.at[o - 1], left.at[9], rc.at[0], (peers[o], gz))
    settle(got5, rc.at[0])
    for o in range(1, ny):
        total = total + got5[o - 1]
    last[gz] = total * scale
    for o in range(1, nz):
        send(last.at[gz], last.at[gz], left.at[10], rd.at[0], (gy, planes[o]))
    settle(last.at[pl.ds(0, nz - 1)], rd.at[0])
    done = pltpu.make_async_copy(last, out_ref, io.at[2])
    done.start()
    gone = [
        got1, got2, got3, full.at[pl.ds(0, (depth - 1) * groups * small)],
        full.at[pl.ds(0, depth * (nz - 1) * groups * small)], full.at[pl.ds(0, rows_full // 2)], raw.at[pl.ds(0, ny - 1)], whole_once, got4, got5,
        last.at[pl.ds(0, nz - 1)],
    ]
    if twice:
        gone += [more.at[pl.ds(0, len(twice))], whole_twice]
    for k, view in enumerate(gone):
        settle(view, left.at[k])
    leave.wait()
    done.wait()


def deliver_kernel(a_ref, b_ref, c_ref, d_ref):
    c_ref[...] = a_ref[...]
    d_ref[...] = b_ref[...]


def deliver(a, b):
    shape = jax.ShapeDtypeStruct
    return pl.pallas_call(
        deliver_kernel, out_shape=(shape(a.shape, a.dtype), shape(b.shape, b.dtype)),
        in_specs=[VMEM, VMEM], out_specs=(VMEM, VMEM), name="deliver",
    )(a, b)


def whole(state_field, start_factor, divisor):
    ny, nz = lax.axis_size("gy"), lax.axis_size("gz")
    nv, nk, jb, n1 = state_field.shape
    r1 = start_factor.shape[1]
    half = nv * nk // 2
    rows = half // ny * jb
    halves = state_field.reshape(2, half * jb, n1)
    n = n1 // LANES
    groups = n * (n + 1) // 4
    depth = ny // 2
    small = LANES // (nz * depth)
    count = len(batches_of(groups))
    q, j2 = jb // nz, ny * jb
    f32, bf16 = jnp.float32, jnp.bfloat16
    dma = pltpu.SemaphoreType.DMA
    vmem = pltpu.VMEM
    factor, out = pl.pallas_call(
        functools.partial(whole_kernel, ny, nz, jb, 1.0 / divisor),
        out_shape=(jax.ShapeDtypeStruct((r1, n1), f32), jax.ShapeDtypeStruct((nz, q, j2), f32)),
        in_specs=[ANY, ANY], out_specs=(ANY, ANY),
        scratch_shapes=[
            dma((3,)),
            vmem((ny, 2, rows, n1), bf16),
            vmem((2 * groups, LANES, LANES), f32),
            vmem((groups, LANES, LANES), f32),
            vmem((groups, LANES, LANES), f32),
            vmem((groups, nz - 1, LANES // nz, LANES), f32),
            vmem((groups, LANES // nz, LANES), f32),
            vmem((groups, depth - 1, small, LANES), f32),
            vmem((groups * small * ny * nz, LANES), f32),
            vmem((n1, n1), bf16), vmem((n1, n1), bf16), vmem((n1, n1), bf16),
            vmem((r1, n1), f32),
            vmem((2, n1, LANES), bf16),
            vmem((ny, 2, jb, n1), bf16),
            vmem((ny, 2, jb, n1), bf16),
            vmem((ny, rows, LANES), bf16),
            vmem((ny, rows, LANES), bf16),
            vmem((ny, nz, q, j2), f32),
            vmem((ny, nz - 1, q, j2), f32),
            vmem((ny - 1, q, j2), f32),
            vmem((ny - 1, q, j2), f32),
            vmem((nz, q, j2), f32),
            dma((2,)), dma((13,)), dma((groups,)), dma((groups,)), dma((count,)), dma((count, depth - 1)),
            dma((count, depth)),
            dma((1,)), dma((2,)), dma((2,)), dma((ny,)), dma((1,)), dma((1,)),
        ],
        compiler_params=pltpu.CompilerParams(
            collective_id=1, has_side_effects=True, vmem_limit_bytes=56 * 2**20
        ),
        name="whole",
    )(halves, start_factor.T)
    factor, out = deliver(factor, out)
    return factor.T, out.reshape(jb, j2)


def second_gram_plain(state_field, narrow, divisor):
    shrunk = jnp.einsum(
        "vkji,ir->jvkr", state_field, narrow, preferred_element_type=jnp.float32
    ).astype(jnp.bfloat16)
    matrix = shrunk.reshape(shrunk.shape[0], -1)
    columns = lax.all_to_all(matrix, "gy", split_axis=1, concat_axis=0, tiled=True)
    partial_two = lax.psum_scatter(dot(columns, columns, NT), "gy", scatter_dimension=0, tiled=True)
    return lax.psum(partial_two, "gz") / divisor


def per_device(state_field, start_factor):
    ny, nz = lax.axis_size("gy"), lax.axis_size("gz")
    nv, nk, jb, n1 = state_field.shape
    r1 = start_factor.shape[1]
    divisor = nv * nk * nz * r1
    halves = (nv * nk) % (2 * ny) == 0 and jb % (8 * nz) == 0 and 2 * r1 == LANES
    if halves and n1 % (4 * LANES) == 0 and ny % 4 == 0 and LANES % (4 * ny * nz) == 0:
        return whole(state_field, start_factor, divisor)
    flattened = state_field.reshape(-1, n1)
    partial_value = dot(flattened, flattened, (((0,), (0,)), ((), ())))
    factor_one = iterate(sum_over_devices(partial_value), start_factor)
    return (factor_one, second_gram_plain(state_field, factor_one.astype(jnp.bfloat16), divisor))


def solution(mesh):
    placed = (P(None, "gz", "gy", None), P())
    return jax.shard_map(
        per_device, mesh=mesh, in_specs=placed, out_specs=(P(), P("gy", None)), check_vma=False
    )
```

```python
import functools

import jax
import jax.numpy as jnp
from jax import lax
from jax.experimental import pallas as pl
from jax.experimental.pallas import tpu as pltpu
from jax.sharding import PartitionSpec as P

ITERS = 6
EARLY = (4, 5)
TWICE = (4, 5)
MESH = pl.DeviceIdType.MESH
LANES = 128
VMEM = pl.BlockSpec(memory_space=pltpu.VMEM)
ANY = pl.BlockSpec(memory_space=pl.ANY)
NT = (((1,), (1,)), ((), ()))


def greet(partners):
    barrier = pltpu.get_barrier_semaphore()
    for partner in partners:
        pl.semaphore_signal(barrier, inc=1, device_id=partner, device_id_type=MESH)
    pl.semaphore_wait(barrier, len(partners))


def send(src, dst, send_sem, recv_sem, device):
    copy = pltpu.make_async_remote_copy(
        src_ref=src, dst_ref=dst, send_sem=send_sem, recv_sem=recv_sem,
        device_id=device, device_id_type=MESH,
    )
    copy.start()
    return copy


def settle(view, sem):
    pltpu.make_async_copy(view, view, sem).wait()


def sum_kernel(ny, nz, chunk, g_ref, out_ref, packed, got1, held, got2, mid, got3, full,
               s1, r1, s2, r2, s3, r3, s4, r4, s5, r5, s6, r6):
    gy, gz = lax.axis_index("gy"), lax.axis_index("gz")
    depth = ny // 2
    zi, core = gy // 2, gy % 2
    rows2 = depth * chunk
    partner = (gy + 1 - 2 * core, gz)
    planes = [lax.rem(gz + o, nz) for o in range(nz)]
    stacks = [lax.rem(zi + o, depth) for o in range(depth)]

    def part(half, g):
        return pl.ds(pl.multiple_of((half * nz + g) * rows2, 8), rows2)

    n = g_ref.shape[0] // LANES
    blocks = [(i, j) for i in range(n) for j in range(i, n)]
    for k, (i, j) in enumerate(blocks):
        packed[k * LANES:(k + 1) * LANES, :] = g_ref[i * LANES:(i + 1) * LANES, j * LANES:(j + 1) * LANES]
    used = len(blocks) * LANES
    if used < packed.shape[0]:
        packed[used:, :] = jnp.zeros((packed.shape[0] - used, LANES), jnp.float32)

    greet([partner] + [(gy, g) for g in planes[1:]] + [(2 * q + core, gz) for q in stacks[1:]])

    order = list(range(1, nz)) + [0]
    copies = []
    first = {}
    for o in order:
        first[o] = send(packed.at[part(1 - core, planes[o])], got1.at[o], s1.at[o], r1.at[o], partner)
    second = {}
    for o in order:
        first[o].wait_recv()
        held[o] = packed[part(core, planes[o]), :] + got1[o]
        if o:
            second[o] = send(held.at[o], got2.at[o], s2.at[o], r2.at[o], (gy, planes[o]))
    total = held[0]
    for o in range(1, nz):
        second[o].wait_recv()
        total = total + got2[o]
    mid[...] = total
    third = {}
    for o in range(1, depth):
        rows = pl.ds(pl.multiple_of(stacks[o] * chunk, 8), chunk)
        third[o] = send(mid.at[rows], got3.at[o], s3.at[o], r3.at[o], (2 * stacks[o] + core, gz))
    piece = mid[pl.ds(pl.multiple_of(zi * chunk, 8), chunk), :]
    for o in range(1, depth):
        third[o].wait_recv()
        piece = piece + got3[o]
    mine = pl.ds(pl.multiple_of((core * nz + gz) * rows2 + zi * chunk, 8), chunk)
    full[mine, :] = piece
    fourth = {}
    for o in range(1, depth):
        fourth[o] = send(full.at[mine], full.at[mine], s4.at[o], r4.at[o], (2 * stacks[o] + core, gz))
    for o in range(1, depth):
        fourth[o].wait_recv()
    own = part(core, gz)
    fifth, sixth = {}, {}
    for o in range(1, nz):
        fifth[o] = send(full.at[own], full.at[own], s5.at[o], r5.at[o], (gy, planes[o]))
    sixth[0] = send(full.at[own], full.at[own], s6.at[0], r6.at[0], partner)
    for o in range(1, nz):
        fifth[o].wait_recv()
        came = part(core, lax.rem(gz + nz - o, nz))
        sixth[o] = send(full.at[came], full.at[came], s6.at[o], r6.at[o], partner)
    for o in range(nz):
        sixth[o].wait_recv()
    for group in (first, second, third, fourth, fifth, sixth):
        for copy in group.values():
            copy.wait_send()
    for k, (i, j) in enumerate(blocks):
        block = full[k * LANES:(k + 1) * LANES, :]
        out_ref[i * LANES:(i + 1) * LANES, j * LANES:(j + 1) * LANES] = block
        if i != j:
            out_ref[j * LANES:(j + 1) * LANES, i * LANES:(i + 1) * LANES] = block.T


def sum_over_devices(partial_gram):
    ny, nz = lax.axis_size("gy"), lax.axis_size("gz")
    n = partial_gram.shape[0] // LANES
    used = n * (n + 1) // 2 * LANES
    devices = ny * nz
    chunk = -(-used // (8 * devices)) * 8
    depth = ny // 2
    rows2 = depth * chunk
    f32 = jnp.float32
    dma = pltpu.SemaphoreType.DMA
    return pl.pallas_call(
        functools.partial(sum_kernel, ny, nz, chunk),
        out_shape=jax.ShapeDtypeStruct(partial_gram.shape, f32),
        in_specs=[VMEM], out_specs=VMEM,
        scratch_shapes=[
            pltpu.VMEM((chunk * devices, LANES), f32),
            pltpu.VMEM((nz, rows2, LANES), f32),
            pltpu.VMEM((nz, rows2, LANES), f32),
            pltpu.VMEM((nz, rows2, LANES), f32),
            pltpu.VMEM((rows2, LANES), f32),
            pltpu.VMEM((depth, chunk, LANES), f32),
            pltpu.VMEM((chunk * devices, LANES), f32),
        ] + [dma((nz,))] * 4 + [dma((depth,))] * 4 + [dma((nz,))] * 4,
        compiler_params=pltpu.CompilerParams(collective_id=0, has_side_effects=True),
        name="sum_gram",
    )(partial_gram)


def split(value):
    high = value.astype(jnp.bfloat16)
    rest = value - high.astype(jnp.float32)
    mid = rest.astype(jnp.bfloat16)
    low = (rest - mid.astype(jnp.float32)).astype(jnp.bfloat16)
    return high, mid, low


def dot(a, b, dims=(((1,), (0,)), ((), ()))):
    return lax.dot_general(a, b, dims, preferred_element_type=jnp.float32)


def rows_of(tile, k):
    return jnp.broadcast_to(tile[k:k + 1, :], tile.shape)


def lanes_of(tile, k):
    return jnp.take_along_axis(tile, jnp.full(tile.shape, k, jnp.int32), axis=1, mode="promise_in_bounds")


def inverse_lower(c):
    r1 = c.shape[0]
    nb = r1 // 8
    wide = 2 * r1
    row = lax.broadcasted_iota(jnp.int32, (r1, r1), 0)
    col = lax.broadcasted_iota(jnp.int32, (r1, r1), 1)
    whole = jnp.concatenate([c, (row == col).astype(jnp.float32)], axis=1)
    m = [whole[8 * i:8 * i + 8, :] for i in range(nb)]
    sub = lax.broadcasted_iota(jnp.int32, (8, wide), 0)
    lane = lax.broadcasted_iota(jnp.int32, (8, wide), 1)
    diag = [lanes_of(m[0], k) for k in range(8)]
    root = lax.rsqrt(rows_of(diag[0], 0))
    unit = root * root
    scale = jnp.where(lane < r1, unit, root)
    diag = [v * unit for v in diag]
    result = []
    for b in range(nb):
        cols = [[diag[k]] + [lanes_of(m[i], 8 * b + k) for i in range(b + 1, nb)] for k in range(8)]
        after = [lanes_of(m[b + 1], 8 * (b + 1) + k) for k in range(8)] if b + 1 < nb else []
        if b == 0:
            cols = [v[:1] + [x * unit for x in v[1:]] for v in cols]
            after = [x * unit for x in after]
            m = [x * scale for x in m]
        done = None
        for k in range(0, 8, 2):
            x, y = cols[k], cols[k + 1]
            p, q = x[0], y[0]
            a, e, d = rows_of(p, k), rows_of(p, k + 1), rows_of(q, k + 1)
            r = lax.rsqrt(a * d - e * e)
            inv = r * r
            g0, h0 = d * p - e * q, a * q - e * p
            ai, ei, di = a * inv, e * inv, d * inv
            ratio = [(g0 * inv, h0 * inv)]
            ratio += [(di * v - ei * w, ai * w - ei * v) for v, w in zip(x[1:], y[1:])]
            for k2 in range(k + 2, 8):
                s, t = rows_of(p, k2), rows_of(q, k2)
                new = [v - (g * s + h * t) for v, (g, h) in zip(cols[k2], ratio)]
                if k2 < k + 4:
                    new[0] = cols[k2][0] - (g0 * s + h0 * t) * inv
                cols[k2] = new
            for k2, v in enumerate(after):
                g, h = ratio[1]
                after[k2] = v - (g * rows_of(x[1], k2) + h * rows_of(y[1], k2))
            u, w = rows_of(m[b], k), rows_of(m[b], k + 1)
            ra = lax.rsqrt(a)
            fresh = jnp.where(sub == k, u * ra, (w - (e * (ra * ra)) * u) * (a * ra * r))
            done = fresh if done is None else jnp.where(sub < k, done, fresh)
            for i in range(b, nb):
                g, h = ratio[i - b]
                m[i] = m[i] - (g * u + h * w)
        result.append(done[:, r1:])
        diag = after
    return jnp.concatenate(result, axis=0)


def times_gram(a1, a2, a3, g1, g2, g3):
    r1 = a1.shape[0]
    t1 = dot(jnp.concatenate([a1, a2, a3], axis=0), g1[...])
    t2 = dot(jnp.concatenate([a1, a2], axis=0), g2[...])
    t3 = dot(a1, g3[...])
    return t1[:r1] + ((t1[r1:2 * r1] + t2[:r1]) + (t1[2 * r1:] + t2[r1:] + t3))


def iteration(g1, g2, g3, held, step, carry):
    r1 = held.shape[0]
    a1, a2, a3 = split(held[...])
    p1 = dot(jnp.concatenate([a1, a2, a3], axis=0), a1, NT)
    p2 = dot(jnp.concatenate([a1, a2], axis=0), a2, NT)
    p3 = dot(a1, a3, NT)
    c = p1[:r1] + (p2[:r1] + p1[r1:2 * r1] + (p2[r1:] + p3 + p1[2 * r1:]))
    last = step == ITERS - 1
    b = split(times_gram(a1, a2, a3, g1, g2, g3))
    stack = jnp.concatenate([jnp.where(last, x, y) for x, y in zip((a1, a2, a3), b)], axis=0)
    w1, w2, w3 = split(inverse_lower(c))
    none = jnp.zeros_like(w1)
    t = dot(
        jnp.concatenate(
            [
                jnp.concatenate([w1, w1, w1], axis=1),
                jnp.concatenate([w2, w2, none], axis=1),
                jnp.concatenate([w3, none, none], axis=1),
            ],
            axis=0,
        ),
        stack,
    )
    held[...] = t[:r1] + (t[r1:2 * r1] + t[2 * r1:])
    return carry


def iterate_kernel(g_ref, f_ref, out_ref, g1, g2, g3, held):
    g1[...], g2[...], g3[...] = split(g_ref[...])
    held[...] = times_gram(*split(f_ref[...].T), g1, g2, g3)
    lax.fori_loop(0, ITERS, functools.partial(iteration, g1, g2, g3, held), 0)
    out_ref[...] = held[...].T


def iterate(mode_gram, start_factor):
    n, r1 = start_factor.shape
    return pl.pallas_call(
        iterate_kernel,
        out_shape=jax.ShapeDtypeStruct((n, r1), jnp.float32),
        in_specs=[VMEM, VMEM], out_specs=VMEM,
        scratch_shapes=[pltpu.VMEM((n, n), jnp.bfloat16)] * 3 + [pltpu.VMEM((r1, n), jnp.float32)],
        name="subspace",
    )(mode_gram, start_factor)


def batches_of(groups):
    early = groups - 2
    return [list(range(early)), list(range(early, groups))] if early > 0 else [list(range(groups))]


def tiles_of(n):
    return [(i, j) for i in range(n) for j in range(i + 1, n)] + [(i, i) for i in range(n)]


def blocks_of(n):
    blocks = []
    for i, j in tiles_of(n // 2):
        blocks += [(2 * i + a, 2 * j + b) for a in range(2) for b in range(2) if i < j or a <= b]
    return blocks


def whole_kernel(ny, nz, jb, scale, x_ref, f_ref, factor_ref, out_ref,
                 io, xs, packed, got1, held, got2, mid, got3, full, g1, g2, g3, basis, weights,
                 raw, more, mine, z, gram, got4, part, got5, last,
                 xsem, left, r1, r2, r3, r4, r5, r6, rr, ra, rb, rc, rd):
    gy, gz = lax.axis_index("gy"), lax.axis_index("gz")
    depth = ny // 2
    zi, core = gy // 2, gy % 2
    partner = (gy + 1 - 2 * core, gz)
    planes = [lax.rem(gz + o, nz) for o in range(nz)]
    stacks = [lax.rem(zi + p, depth) for p in range(depth)]
    peers = [lax.rem(gy + o, ny) for o in range(ny)]
    rows = mine.shape[1]
    soon = [o for o in EARLY if 0 < o < ny]
    twice = [o for o in TWICE if 0 < o < ny]
    once = [o for o in range(1, ny) if o not in twice]
    first_rows, next_rows = pl.ds(0, jb), pl.ds(jb, jb)
    n1 = x_ref.shape[2]

    barrier = pltpu.get_barrier_semaphore()
    greeted = [(p, gz) for p in peers[1:]] + [(gy, g) for g in planes[1:]]
    for device in greeted:
        pl.semaphore_signal(barrier, inc=1, device_id=device, device_id_type=MESH)

    def load(o):
        src = x_ref.at[:, pl.ds(pl.multiple_of(peers[o] * rows, 8), rows)]
        return pltpu.make_async_copy(src, xs.at[o], xsem.at[2 * o // ny])

    loads = [load(o) for o in range(ny)]
    for copy in loads:
        copy.start()
    start = pltpu.make_async_copy(f_ref, basis, io.at[0])
    start.start()

    size = 2 * LANES
    n = n1 // LANES
    blocks = blocks_of(n)
    groups = len(blocks) // 2
    order = {block: k for k, block in enumerate(blocks)}
    wide_piece = LANES // nz
    small = wide_piece // depth
    batches = batches_of(groups)
    batch_of = {k: b for b, batch in enumerate(batches) for k in batch}

    def add_tile(i, j, low, high, start):
        deep = (high - low) * 2 * rows
        left = xs[low:high, :, :, i * size:(i + 1) * size].reshape(deep, size)
        right = xs[low:high, :, :, j * size:(j + 1) * size].reshape(deep, size)
        value = dot(left, right, (((0,), (0,)), ((), ())))
        for a in range(2):
            for b in range(2):
                k = order.get((2 * i + a, 2 * j + b))
                if k is not None:
                    block = value[a * LANES:(a + 1) * LANES, b * LANES:(b + 1) * LANES]
                    if start:
                        packed[k] = block
                    else:
                        packed[k] += block

    def pair_up(k):
        send(packed.at[2 * k + 1 - core], got1.at[k], left.at[0], r1.at[k], partner)

    def spread_plane(k):
        settle(got1.at[k], r1.at[k])
        held[k] = packed[2 * k + core] + got1[k]
        for o in range(1, nz):
            part_o = pl.ds(pl.multiple_of(planes[o] * wide_piece, 8), wide_piece)
            send(held.at[k, part_o], got2.at[k, o - 1], left.at[1], r2.at[k], (gy, planes[o]))

    tiles = tiles_of(n // 2)
    half_way = ny // 2
    for low in (0, half_way):
        settle(xs.at[pl.ds(low, half_way)], xsem.at[low // half_way])
        add_tile(*tiles[0], low, low + half_way, low == 0)
    pl.semaphore_wait(barrier, len(greeted))
    def send_raw(o):
        send(xs.at[o, :, first_rows], raw.at[gy], left.at[6], rr.at[0], (peers[o], gz))

    for k in range(2):
        pair_up(k)
    for o in soon:
        send_raw(o)
    for i, j in tiles[1:]:
        for low in (0, half_way):
            add_tile(i, j, low, low + half_way, low == 0)
    for k in range(2, groups):
        pair_up(k)
    for k in range(groups):
        spread_plane(k)
    for k in range(groups):
        total = held[k, pl.ds(pl.multiple_of(gz * wide_piece, 8), wide_piece), :]
        settle(got2.at[k], r2.at[k])
        for o in range(1, nz):
            total = total + got2[k, o - 1]
        mid[k] = total
        for p in range(1, depth):
            part_p = pl.ds(pl.multiple_of(stacks[p] * small, 8), small)
            send(mid.at[k, part_p], got3.at[k, p - 1], left.at[2], r3.at[batch_of[k]], (2 * stacks[p] + core, gz))

    pieces = 2 * depth * nz

    def span(b, half, q, g=0, count=nz):
        chunk = len(batches[b]) * small
        start = batches[b][0] * small * pieces
        return pl.ds(pl.multiple_of(start + ((half * depth + q) * nz + g) * chunk, 8), count * chunk)

    def some(b, count):
        return full.at[pl.ds(0, count * len(batches[b]) * small)]

    for b, batch in enumerate(batches):
        settle(got3.at[pl.ds(batch[0], len(batch))], r3.at[b])
        total = mid[batch[0]:batch[-1] + 1, pl.ds(pl.multiple_of(zi * small, 8), small), :]
        for p in range(1, depth):
            total = total + got3[batch[0]:batch[-1] + 1, p - 1]
        own = span(b, core, zi, gz, 1)
        full[own, :] = total.reshape(len(batch) * small, LANES)
        for p in range(1, depth):
            send(full.at[own], full.at[own], left.at[3], r4.at[b, p - 1], (2 * stacks[p] + core, gz))
    came = [lax.rem(zi + depth - p, depth) for p in range(depth)]
    for b in range(len(batches)):
        for p in range(depth):
            if p:
                settle(some(b, 1), r4.at[b, p - 1])
            here = span(b, core, came[p], gz, 1)
            for o in range(1, nz):
                send(full.at[here], full.at[here], left.at[4], r5.at[b, p], (gy, planes[o]))
    for b in range(len(batches)):
        for p in range(depth):
            settle(some(b, nz - 1), r5.at[b, p])
            here = span(b, core, came[p])
            send(full.at[here], full.at[here], left.at[5], r6.at[0], partner)
    rows_full = pieces * groups * small
    settle(full.at[pl.ds(0, rows_full // 2)], r6.at[0])

    far = list(range(ny // 2, ny)) + list(range(ny // 2 - 1, 0, -1))
    for o in far:
        if o not in soon:
            send_raw(o)
    for o in twice:
        send(xs.at[o, :, next_rows], more.at[gy], left.at[11], rr.at[1], (peers[o], gz))

    for k, (i, j) in enumerate(blocks):
        batch = batches[batch_of[k // 2]]
        chunk = len(batch) * small
        at = batch[0] * small * pieces + (k // 2 - batch[0]) * small
        rows_k = [at + ((k % 2 * depth + q) * nz + g) * chunk for g in range(nz) for q in range(depth)]
        block = jnp.concatenate([full[row:row + small, :] for row in rows_k], axis=0)
        for a, b, value in ((i, j, block), (j, i, block.T))[:1 if i == j else 2]:
            where = (slice(a * LANES, (a + 1) * LANES), slice(b * LANES, (b + 1) * LANES))
            g1[where], g2[where], g3[where] = split(value)
    start.wait()
    basis[...] = times_gram(*split(basis[...]), g1, g2, g3)
    lax.fori_loop(0, ITERS, functools.partial(iteration, g1, g2, g3, basis), 0)
    factor = basis[...]
    factor_ref[...] = factor
    narrow = factor.T.astype(jnp.bfloat16)
    empty = jnp.zeros_like(narrow)
    weights[0] = jnp.concatenate([narrow, empty], axis=1)
    weights[1] = jnp.concatenate([empty, narrow], axis=1)

    def project(pair):
        return (dot(pair[0], weights[0]) + dot(pair[1], weights[1])).astype(jnp.bfloat16)

    ranges = {o: pl.ds(2 * jb, rows - 2 * jb) if o in twice else pl.ds(jb, rows - jb) for o in far}
    for o in far:
        late, kind = ranges[o], int(o in twice)
        mine[o, late] = project(xs[o, :, late])
        send(mine.at[o, late], z.at[gy, late], left.at[12 if kind else 7], ra.at[kind], (peers[o], gz))
    z[gy] = project(xs[0])
    settle(raw.at[pl.ds(0, ny - 1)], rr.at[0])
    for o in range(1, ny):
        z[peers[o], first_rows] = project(raw[peers[o]])
    if twice:
        settle(more.at[pl.ds(0, len(twice))], rr.at[1])
    for o in twice:
        source = lax.rem(gy + ny - o, ny)
        z[source, next_rows] = project(more[source])
    whole_once = z.at[pl.ds(0, len(once)), pl.ds(jb, rows - jb)]
    settle(whole_once, ra.at[0])
    whole_twice = z.at[pl.ds(0, max(len(twice), 1)), pl.ds(2 * jb, rows - 2 * jb)]
    if twice:
        settle(whole_twice, ra.at[1])
    wide = jnp.concatenate(
        [z[:, t * jb:(t + 1) * jb, :].reshape(ny * jb, LANES) for t in range(rows // jb)], axis=1
    )
    gram[...] = dot(wide, wide, NT).reshape(gram.shape)
    far = far + [0]
    for o in far:
        for g in range(1, nz):
            send(gram.at[peers[o], planes[g]], got4.at[o, g - 1], left.at[8], rb.at[o], (gy, planes[g]))
    for o in far:
        settle(got4.at[o], rb.at[o])
        total = gram[peers[o], gz]
        for g in range(1, nz):
            total = total + got4[o, g - 1]
        if o:
            part[o - 1] = total
            send(part.at[o - 1], got5.at[o - 1], left.at[9], rc.at[0], (peers[o], gz))
    settle(got5, rc.at[0])
    for o in range(1, ny):
        total = total + got5[o - 1]
    last[gz] = total * scale
    for o in range(1, nz):
        send(last.at[gz], last.at[gz], left.at[10], rd.at[0], (gy, planes[o]))
    settle(last.at[pl.ds(0, nz - 1)], rd.at[0])
    out_ref[...] = last[...]
    gone = [
        got1, got2, got3, full.at[pl.ds(0, (depth - 1) * groups * small)],
        full.at[pl.ds(0, depth * (nz - 1) * groups * small)], full.at[pl.ds(0, rows_full // 2)], raw.at[pl.ds(0, ny - 1)], whole_once, got4, got5,
        last.at[pl.ds(0, nz - 1)],
    ]
    if twice:
        gone += [more.at[pl.ds(0, len(twice))], whole_twice]
    for k, view in enumerate(gone):
        settle(view, left.at[k])


def deliver_kernel(a_ref, b_ref, c_ref, d_ref, sem):
    left = [pltpu.make_async_copy(a_ref, c_ref, sem.at[0]), pltpu.make_async_copy(b_ref, d_ref, sem.at[1])]
    for copy in left:
        copy.start()
    for copy in left:
        copy.wait()


def deliver(a, b):
    shape = jax.ShapeDtypeStruct
    return pl.pallas_call(
        deliver_kernel, out_shape=(shape(a.shape, a.dtype), shape(b.shape, b.dtype)),
        in_specs=[VMEM, VMEM], out_specs=(ANY, ANY), name="deliver",
        scratch_shapes=[pltpu.SemaphoreType.DMA((2,))],
    )(a, b)


def whole(state_field, start_factor, divisor):
    ny, nz = lax.axis_size("gy"), lax.axis_size("gz")
    nv, nk, jb, n1 = state_field.shape
    r1 = start_factor.shape[1]
    half = nv * nk // 2
    rows = half // ny * jb
    halves = state_field.reshape(2, half * jb, n1)
    n = n1 // LANES
    groups = n * (n + 1) // 4
    depth = ny // 2
    small = LANES // (nz * depth)
    count = len(batches_of(groups))
    q, j2 = jb // nz, ny * jb
    f32, bf16 = jnp.float32, jnp.bfloat16
    dma = pltpu.SemaphoreType.DMA
    vmem = pltpu.VMEM
    factor, out = pl.pallas_call(
        functools.partial(whole_kernel, ny, nz, jb, 1.0 / divisor),
        out_shape=(pltpu.VMEM((r1, n1), f32), pltpu.VMEM((nz, q, j2), f32)),
        in_specs=[ANY, ANY], out_specs=(VMEM, VMEM),
        scratch_shapes=[
            dma((1,)),
            vmem((ny, 2, rows, n1), bf16),
            vmem((2 * groups, LANES, LANES), f32),
            vmem((groups, LANES, LANES), f32),
            vmem((groups, LANES, LANES), f32),
            vmem((groups, nz - 1, LANES // nz, LANES), f32),
            vmem((groups, LANES // nz, LANES), f32),
            vmem((groups, depth - 1, small, LANES), f32),
            vmem((groups * small * ny * nz, LANES), f32),
            vmem((n1, n1), bf16), vmem((n1, n1), bf16), vmem((n1, n1), bf16),
            vmem((r1, n1), f32),
            vmem((2, n1, LANES), bf16),
            vmem((ny, 2, jb, n1), bf16),
            vmem((ny, 2, jb, n1), bf16),
            vmem((ny, rows, LANES), bf16),
            vmem((ny, rows, LANES), bf16),
            vmem((ny, nz, q, j2), f32),
            vmem((ny, nz - 1, q, j2), f32),
            vmem((ny - 1, q, j2), f32),
            vmem((ny - 1, q, j2), f32),
            vmem((nz, q, j2), f32),
            dma((2,)), dma((13,)), dma((groups,)), dma((groups,)), dma((count,)), dma((count, depth - 1)),
            dma((count, depth)),
            dma((1,)), dma((2,)), dma((2,)), dma((ny,)), dma((1,)), dma((1,)),
        ],
        compiler_params=pltpu.CompilerParams(
            collective_id=1, has_side_effects=True, vmem_limit_bytes=56 * 2**20
        ),
        name="whole",
    )(halves, start_factor.T)
    factor = pltpu.with_memory_space_constraint(factor, pltpu.VMEM)
    out = pltpu.with_memory_space_constraint(out, pltpu.VMEM)
    factor, out = deliver(factor, out)
    return factor.T, out.reshape(jb, j2)


def second_gram_plain(state_field, narrow, divisor):
    shrunk = jnp.einsum(
        "vkji,ir->jvkr", state_field, narrow, preferred_element_type=jnp.float32
    ).astype(jnp.bfloat16)
    matrix = shrunk.reshape(shrunk.shape[0], -1)
    columns = lax.all_to_all(matrix, "gy", split_axis=1, concat_axis=0, tiled=True)
    partial_two = lax.psum_scatter(dot(columns, columns, NT), "gy", scatter_dimension=0, tiled=True)
    return lax.psum(partial_two, "gz") / divisor


def per_device(state_field, start_factor):
    ny, nz = lax.axis_size("gy"), lax.axis_size("gz")
    nv, nk, jb, n1 = state_field.shape
    r1 = start_factor.shape[1]
    divisor = nv * nk * nz * r1
    halves = (nv * nk) % (2 * ny) == 0 and jb % (8 * nz) == 0 and 2 * r1 == LANES
    if halves and n1 % (4 * LANES) == 0 and ny % 4 == 0 and LANES % (4 * ny * nz) == 0:
        return whole(state_field, start_factor, divisor)
    flattened = state_field.reshape(-1, n1)
    partial_value = dot(flattened, flattened, (((0,), (0,)), ((), ())))
    factor_one = iterate(sum_over_devices(partial_value), start_factor)
    return (factor_one, second_gram_plain(state_field, factor_one.astype(jnp.bfloat16), divisor))


def solution(mesh):
    placed = (P(None, "gz", "gy", None), P())
    return jax.shard_map(
        per_device, mesh=mesh, in_specs=placed, out_specs=(P(), P("gy", None)), check_vma=False
    )
```
